256 devices in a mesh: fsdp: 16 (over x, z_lo, core), pair: 16 (over z_hi, y).
Axes of the slice: x: 4, y: 4, z: 8 (z_hi: 4, z_lo: 2; z = z_hi * 2 + z_lo), core: 2. Of those that a mesh axis runs over, the one named last changes fastest.
Arguments:
- tokens: bfloat16 [32768, 8192], P('pair', 'fsdp'), may hold values from -6 to 6
- cotangent: bfloat16 [32768, 1024], P('pair', 'fsdp'), may hold values from -6 to 6
- value_weight: bfloat16 [8192, 1024], P('fsdp'), may hold values from -0.0625 to 0.0625
- adapter_down: bfloat16 [48, 8192, 128], P(None, 'fsdp'), may hold values from -0.0625 to 0.0625
- adapter_up: bfloat16 [48, 128, 1024], P(None, None, 'fsdp'), may hold values from -0.5 to 0.5
- pair_ids: int32 [64], P('pair'), may hold values from 0 to 47
- ranks: int32 [48], replicated, may hold values from 16 to 128, as said below
Outputs:
- input_grad: bfloat16 [32768, 8192], P('pair', 'fsdp')
- down_grad: bfloat16 [48, 8192, 128], P('pair', 'fsdp')
- up_grad: bfloat16 [48, 128, 1024], P('pair', None, 'fsdp')
The draws below stay inside these ranges and needn't reach their ends.
Inputs may be any that keep to these rules, and one draw needn't show every extreme that they name: `ranks`: each rank is 128, 64, 32 or 16; both ends occur in every draw.
All inputs are finite; a program needn't handle non-finite values.
Results may differ from the reference program's by a relative error of at most 0.022.
Values may be sent and summed in bfloat16 or wider, within the bound.
A program may use at most 128 MiB of HBM per device.

```python
import math
import jax
import jax.numpy as jnp
import numpy as np
from jax import lax

D = 8192
NPAIR = 48
RMAX = 128
BLOCK = 512
TOKB = 2048
KV = 1024
TOKENS = 32768
NBLOCKS = 64
N_PAIR = 16


def draw_ranks(key, part):
    first, second = jax.random.split(key)
    level = jax.random.randint(first, (NPAIR,), 0, 4)
    values = RMAX // jnp.power(2, level).astype(jnp.int32)
    places = jax.random.permutation(second, NPAIR)
    values = values.at[places[0]].set(RMAX)
    values = values.at[places[1]].set(RMAX // 8)
    return values.astype(jnp.int32)


def with_ends(array, rng, low, high):
    longest = array.shape.index(max(array.shape))
    spots = []
    for shift in (0, 1):
        where = [jax.random.randint(jax.random.fold_in(rng, axis), (), 0, length) for axis, length in enumerate(array.shape)]
        where[longest] = (where[longest] + shift) % array.shape[longest]
        spots.append(tuple(where))
    return array.at[spots[0]].set(low).at[spots[1]].set(high)


def level_of(stream_key, shape, cuts, least, largest):
    level, own = 1.0, jax.random.fold_in(stream_key, 6)
    for dim, shards_of in cuts:
        draws = jnp.exp(jax.random.uniform(jax.random.fold_in(own, dim), (shards_of,), jnp.float32, least / len(cuts), largest / len(cuts)))
        level = level * jnp.repeat(draws, shape[dim] // shards_of).reshape([-1 if axis == dim else 1 for axis in range(len(shape))])
    return level


def cumulative_ranks(count, skew):
    weights = [(1 << 20) // math.isqrt(rank ** skew) + 1 for rank in range(1, count + 1)]
    scale = 1 + sum(weights) // (1 << 30)
    return np.cumsum(np.array([max(1, weight // scale) for weight in weights]))


def ranked(key, dims, count, lean):
    table = cumulative_ranks(count, lean)
    lot = jax.random.randint(jax.random.fold_in(key, 1), dims, 0, int(table[count - 1]))
    rank = jnp.searchsorted(jnp.asarray(table, jnp.int32), lot, side="right")
    return jax.random.permutation(jax.random.fold_in(key, 2), count)[rank].astype(jnp.int32)


def centred(own_key, dims, scale, most, shards=(), kind=jnp.bfloat16):
    result = scale * jax.random.normal(own_key, dims, jnp.float32)
    if shards:
        result = result * level_of(own_key, dims, shards, -0.22, 0.18)
    return jnp.clip(result, -most, most).astype(kind)


def setup_inputs(seed: int = 0) -> dict:
    splits = jax.random.split(jax.random.key(seed), 8)
    tokens = centred(splits[0], (TOKENS, D), 1.0, 6.0, ((0, 16), (1, 16)))
    cotangent = centred(splits[1], (TOKENS, KV), 1.0, 6.0, ((0, 16), (1, 16)))
    value_weight = centred(splits[2], (D, KV), D ** -0.5, 0.0625, ((0, 16),))
    adapter_down = centred(splits[3], (NPAIR, D, RMAX), D ** -0.5, 0.0625, ((1, 16),))
    adapter_up = centred(splits[4], (NPAIR, RMAX, KV), RMAX ** -0.5, 0.5, ((2, 16),))
    pair_ids = with_ends(ranked(splits[5], (NBLOCKS,), NPAIR, 2), jax.random.fold_in(splits[5], 3), 0, NPAIR - 1).astype(jnp.int32)
    ranks = draw_ranks(jax.random.fold_in(splits[7], 71), 0)
    return {"tokens": tokens, "cotangent": cotangent, "value_weight": value_weight, "adapter_down": adapter_down, "adapter_up": adapter_up, "pair_ids": pair_ids, "ranks": ranks}


def reference(tokens, cotangent, value_weight, adapter_down, adapter_up, pair_ids, ranks):
    block_count = TOKB // BLOCK
    columns = jnp.arange(RMAX, dtype=jnp.int32)
    mask = (columns[None, :] < ranks[:, None]).astype(jnp.float32)
    scale = 32.0 / ranks.astype(jnp.float32)
    norm = 1.0 / math.sqrt(TOKENS)
    weight_f = value_weight.astype(jnp.float32)
    group_x = tokens.reshape(N_PAIR, block_count, BLOCK, D)
    group_c = cotangent.reshape(N_PAIR, block_count, BLOCK, KV)
    group_ids = pair_ids.reshape(N_PAIR, block_count)
    pair_range = jnp.arange(NPAIR, dtype=jnp.int32)

    def step(carry, inputs):
        total_a, total_b = carry
        xs, cs, ids = inputs
        x_f = xs.astype(jnp.float32)
        c_f = cs.astype(jnp.float32)
        selected_down_adapter = adapter_down[ids].astype(jnp.float32)
        b_sel = adapter_up[ids].astype(jnp.float32)
        rows_mask = mask[ids][:, None, :]
        block_offset = scale[ids]
        low = jnp.einsum('btd,bdr->btr', x_f, selected_down_adapter)
        back = jnp.einsum('btk,brk->btr', c_f, b_sel)
        low_b = (low * rows_mask).astype(jnp.bfloat16)
        backward_up_part = (back * rows_mask).astype(jnp.bfloat16)
        frozen_output = jnp.einsum('btk,dk->btd', c_f, weight_f).astype(jnp.bfloat16)
        adapter_output = jnp.einsum('eiz,efz->eif', backward_up_part.astype(jnp.float32), selected_down_adapter)
        input_gradient_total = (frozen_output.astype(jnp.float32) + block_offset[:, None, None] * adapter_output).astype(jnp.bfloat16)
        coef = block_offset * norm
        term_a = jnp.einsum('btd,btr->bdr', x_f, backward_up_part.astype(jnp.float32)) * coef[:, None, None]
        term_b = jnp.einsum('btr,btk->brk', low_b.astype(jnp.float32), c_f) * coef[:, None, None]
        onehot = (ids[:, None] == pair_range[None, :]).astype(jnp.float32)
        part_a = jnp.einsum('bp,bdr->pdr', onehot, term_a).astype(jnp.bfloat16)
        part_b = jnp.einsum('bp,brk->prk', onehot, term_b).astype(jnp.bfloat16)
        return ((total_a + part_a.astype(jnp.float32), total_b + part_b.astype(jnp.float32)), input_gradient_total)
    init = (jnp.zeros((NPAIR, D, RMAX), jnp.float32), jnp.zeros((NPAIR, RMAX, KV), jnp.float32))
    (total_a, total_b), grads = lax.scan(step, init, (group_x, group_c, group_ids))
    input_grad = grads.reshape(TOKENS, D)
    return (input_grad, total_a.astype(jnp.bfloat16), total_b.astype(jnp.bfloat16))
```

```python
import math

import jax
import jax.numpy as jnp
from jax import lax
from jax.experimental import pallas as pl
from jax.experimental.pallas import tpu as pltpu
from jax.sharding import PartitionSpec as P

MESH = pl.DeviceIdType.MESH
BF = jnp.bfloat16
F32 = jnp.float32

NAMES = ["A1", "B1R", "B1L", "B3O", "A2R", "A2L", "B2R", "B2L", "B3L", "B3R", "A3R", "A3L", "B3F", "C0", "CL", "CR", "CF"]
NAMES += ["IR", "IL", "IF"]
NAMES += ["X1R", "X1L", "X2Rb", "X2Lb", "X2Ra", "X2La", "Q1", "Q2", "Q3"]
CHUNKS = [(0, 128), (128, 128), (256, 128), (384, 128), (512, 64)]
for _k in range(len(CHUNKS)):
    NAMES += [n + str(_k) for n in ("YR", "YL", "YFR", "YFL", "Z1R", "Z1L", "Z2Rb", "Z2Lb", "Z2Ra", "Z2La")]
INDEX = {n: i for i, n in enumerate(NAMES)}


def dot(a, b, ca=1, cb=0):
    return lax.dot_general(a, b, (((ca,), (cb,)), ((), ())), preferred_element_type=F32)


def kernel(norm, ids, ranks, tok_h, cot_h, w_h, a_h, b_h, ig_h, dg_h, ug_h,
           G, xv, wv, av, bv, asel, low, backf, backb, YB, ZB, R1, R2, FL, FR,
           V, XR1, XR2, XFL, XFR, XS, QR, idt, Lm, igv, dgv, ugv, ss, rs, ls):
    f = lax.axis_index("fsdp")
    q = lax.axis_index("pair")
    x, z, c = f // 4, (f // 2) % 2, f % 2
    zh, y = q // 4, q % 4
    xr, xl, xo = (x + 1) % 4, (x + 3) % 4, (x + 2) % 4
    yr, yl, yo = (y + 1) % 4, (y + 3) % 4, (y + 2) % 4
    zr, zl = (zh + 1) % 4, (zh + 3) % 4

    def dev(xx, zz, cc):
        return {"fsdp": xx * 4 + zz * 2 + cc}

    def pdev(zz, yy):
        return {"pair": zz * 4 + yy}

    d_z, d_c, d_zc = dev(x, 1 - z, c), dev(x, z, 1 - c), dev(x, 1 - z, 1 - c)
    d_xr, d_xl = dev(xr, z, c), dev(xl, z, c)
    d_yr, d_yl = pdev(zh, yr), pdev(zh, yl)
    d_zr, d_zl = pdev(zr, y), pdev(zl, y)

    sent = []

    def send(name, src, dst, device):
        i = INDEX[name]
        copy = pltpu.make_async_remote_copy(src_ref=src, dst_ref=dst, send_sem=ss.at[i], recv_sem=rs.at[i],
                                            device_id=device, device_id_type=MESH)
        copy.start()
        sent.append(copy)

    def recv(name, dst, device):
        i = INDEX[name]
        pltpu.make_async_remote_copy(src_ref=dst, dst_ref=dst, send_sem=ss.at[i], recv_sem=rs.at[i],
                                     device_id=device, device_id_type=MESH).wait_recv()

    c_cot = pltpu.make_async_copy(cot_h, G.at[x, z, c, :, 0:2048], ls.at[0])
    c_b = pltpu.make_async_copy(b_h, bv, ls.at[1])
    c_x = pltpu.make_async_copy(tok_h, xv, ls.at[2])
    c_a = pltpu.make_async_copy(a_h, av, ls.at[3])
    c_w = pltpu.make_async_copy(w_h, wv, ls.at[4])
    for copy in (c_cot, c_b, c_x, c_a, c_w):
        copy.start()

    barrier = pltpu.get_barrier_semaphore()
    for device in (d_z, d_c, d_zc, d_xr, d_xl, d_yr, d_yl, d_zr, d_zl):
        pl.semaphore_signal(barrier, inc=1, device_id=device, device_id_type=MESH)

    lane = lax.broadcasted_iota(jnp.int32, (8, 256), 1)
    part = (lane >> 4) & 3
    tile = jnp.where(part == 0, ids[0], jnp.where(part == 1, ids[1], jnp.where(part == 2, ids[2], ids[3])))
    idt[y] = tile
    c_b.wait()
    for b in range(4):
        G[x, z, c, :, 2048 + 128 * b:2176 + 128 * b] = bv[ids[b]]
    c_cot.wait()
    pl.semaphore_wait(barrier, 9)

    send("A1", G.at[x, z, c, 0:32], G.at[x, z, c, 0:32], d_z)
    send("B1R", G.at[x, z, c, 32:64], G.at[x, z, c, 32:64], d_xr)
    send("B1L", G.at[x, z, c, 32:64], G.at[x, z, c, 32:64], d_xl)
    send("B3O", G.at[x, z, c, 32:64], G.at[x, z, c, 32:64], d_z)
    send("IR", idt.at[y], idt.at[y], d_yr)
    send("IL", idt.at[y], idt.at[y], d_yl)
    recv("A1", G.at[x, 1 - z, c, 0:32], d_z)
    send("A2R", G.at[x, :, c, 0:32], G.at[x, :, c, 0:32], d_xr)
    send("A2L", G.at[x, :, c, 0:32], G.at[x, :, c, 0:32], d_xl)
    recv("B1R", G.at[xl, z, c, 32:64], d_xl)
    send("B2R", G.at[xl, z, c, 32:48], G.at[xl, z, c, 32:48], d_xr)
    send("B3L", G.at[xl, z, c, 32:64], G.at[xl, z, c, 32:64], d_z)
    recv("B1L", G.at[xr, z, c, 32:64], d_xr)
    send("B2L", G.at[xr, z, c, 48:64], G.at[xr, z, c, 48:64], d_xl)
    send("B3R", G.at[xr, z, c, 32:64], G.at[xr, z, c, 32:64], d_z)
    recv("B3O", G.at[x, 1 - z, c, 32:64], d_z)
    send("C0", G.at[x, :, c], G.at[x, :, c], d_c)
    recv("IR", idt.at[yl], d_yl)
    send("IF", idt.at[yl], idt.at[yl], d_yr)

    c_a.wait()
    c_x.wait()
    for b in range(4):
        asel[b] = av[ids[b]]

    def rank_of(b):
        return ranks[ids[b]]

    def low_body(b, carry):
        value = dot(xv[pl.ds(pl.multiple_of(b * 512, 512), 512), :], asel[b])
        keep = lax.broadcasted_iota(jnp.int32, (512, 128), 1) < rank_of(b)
        low[b] = jnp.where(keep, value, 0.0).astype(BF)
        return carry

    lax.fori_loop(0, 4, low_body, 0)

    def features(g, start, count):
        start = pl.multiple_of(start, 128)
        return G[g, :, :, :, pl.ds(start, count)].reshape(256, count)

    def back_step(g, first):
        def body(b, carry):
            value = dot(features(g, 2048 + 128 * b, 128), features(g, 512 * b, 512), 0, 0)
            if first:
                backf[b] = value
            else:
                backf[b] = backf[b] + value
            return carry
        lax.fori_loop(0, 4, body, 0)

    recv("C0", G.at[x, :, 1 - c], d_c)
    back_step(x, True)
    recv("A2R", G.at[xl, :, c, 0:32], d_xl)
    send("A3R", G.at[xl, :, c, 0:16], G.at[xl, :, c, 0:16], d_xr)
    recv("A2L", G.at[xr, :, c, 0:32], d_xr)
    send("A3L", G.at[xr, :, c, 16:32], G.at[xr, :, c, 16:32], d_xl)
    recv("B2R", G.at[xo, z, c, 32:48], d_xl)
    recv("B2L", G.at[xo, z, c, 48:64], d_xr)
    send("B3F", G.at[xo, z, c, 32:64], G.at[xo, z, c, 32:64], d_z)
    recv("B3L", G.at[xl, 1 - z, c, 32:64], d_z)
    send("CL", G.at[xl, :, c], G.at[xl, :, c], d_c)
    recv("B3R", G.at[xr, 1 - z, c, 32:64], d_z)
    send("CR", G.at[xr, :, c], G.at[xr, :, c], d_c)
    recv("CL", G.at[xl, :, 1 - c], d_c)
    back_step(xl, False)
    recv("CR", G.at[xr, :, 1 - c], d_c)
    back_step(xr, False)
    recv("A3R", G.at[xo, :, c, 0:16], d_xl)
    recv("A3L", G.at[xo, :, c, 16:32], d_xr)
    recv("B3F", G.at[xo, 1 - z, c, 32:64], d_z)
    send("CF", G.at[xo, :, c], G.at[xo, :, c], d_c)

    recv("IL", idt.at[yr], d_yr)
    recv("IF", idt.at[yo], d_yl)
    row = lax.broadcasted_iota(jnp.int32, (192, 256), 0)
    col = lax.broadcasted_iota(jnp.int32, (192, 256), 1)
    slot = row >> 4
    turn = (slot >= 3).astype(jnp.int32) + (slot >= 6).astype(jnp.int32) + (slot >= 9).astype(jnp.int32)
    pair = 3 * (((zh + turn) & 3) * 4 + y) + slot - 3 * turn
    of_block = jnp.zeros((192, 256), jnp.int32)
    for s in range(4):
        of_block = jnp.where((col >> 6) == s, jnp.broadcast_to(idt[s][0:1, :], (192, 256)), of_block)
    hit = jnp.logical_and((row & 15) == (col & 15), of_block == pair)
    Lm[...] = jnp.where(hit, 1.0, 0.0).astype(BF)

    recv("CF", G.at[xo, :, 1 - c], d_c)
    back_step(xo, False)

    def scale_of(b):
        return 32.0 / jnp.broadcast_to(rank_of(b), (1, 128)).astype(F32)

    def mask_body(b, carry):
        keep = lax.broadcasted_iota(jnp.int32, (128, 512), 0) < rank_of(b)
        backb[b] = jnp.where(keep, backf[b], 0.0).astype(BF)
        return carry

    lax.fori_loop(0, 4, mask_body, 0)

    def y_send(k):
        r0, n = CHUNKS[k]
        own = YB.at[y, :, r0:r0 + n]
        send("YR" + str(k), own, own, d_yr)
        send("YL" + str(k), own, own, d_yl)

    def y_forward(k):
        r0, n = CHUNKS[k]
        h = n // 2
        recv("YR" + str(k), YB.at[yl, :, r0:r0 + n], d_yl)
        send("YFR" + str(k), YB.at[yl, :, r0:r0 + h], YB.at[yl, :, r0:r0 + h], d_yr)
        recv("YL" + str(k), YB.at[yr, :, r0:r0 + n], d_yr)
        send("YFL" + str(k), YB.at[yr, :, r0 + h:r0 + n], YB.at[yr, :, r0 + h:r0 + n], d_yl)

    def combine(k):
        r0, n = CHUNKS[k]
        h = n // 2
        recv("YFR" + str(k), YB.at[yo, :, r0:r0 + h], d_yl)
        recv("YFL" + str(k), YB.at[yo, :, r0 + h:r0 + n], d_yr)

        def body(i, carry):
            top = pl.ds(pl.multiple_of(r0 + 32 * i, 16), 16)
            bottom = pl.ds(pl.multiple_of(r0 + 32 * i + 16, 16), 16)
            stack = jnp.concatenate([YB[:, :, top, :].reshape(256, 128), YB[:, :, bottom, :].reshape(256, 128)], axis=1)
            out = dot(Lm[...], stack).astype(BF)
            ZB[:, :, top, :] = out[:, 0:128].reshape(4, 3, 16, 128)
            ZB[:, :, bottom, :] = out[:, 128:256].reshape(4, 3, 16, 128)
            return carry

        lax.fori_loop(0, n // 32, body, 0)
        s0 = r0 // 2
        send("Z1R" + str(k), ZB.at[2, :, r0:r0 + h], R1.at[:, s0:s0 + h], d_zr)
        send("Z1L" + str(k), ZB.at[2, :, r0 + h:r0 + n], R2.at[:, s0:s0 + h], d_zl)
        send("Z2Rb" + str(k), ZB.at[1, :, r0 + h:r0 + n], FL.at[:, r0 + h:r0 + n], d_zr)
        send("Z2Lb" + str(k), ZB.at[3, :, r0:r0 + h], FR.at[:, r0:r0 + h], d_zl)

    def pass_on(k):
        r0, n = CHUNKS[k]
        h = n // 2
        s0 = r0 // 2
        recv("Z1R" + str(k), R1.at[:, s0:s0 + h], d_zl)
        ZB[1, :, r0:r0 + h] = (ZB[1, :, r0:r0 + h].astype(F32) + R1[:, s0:s0 + h].astype(F32)).astype(BF)
        send("Z2Ra" + str(k), ZB.at[1, :, r0:r0 + h], FL.at[:, r0:r0 + h], d_zr)
        recv("Z1L" + str(k), R2.at[:, s0:s0 + h], d_zr)
        ZB[3, :, r0 + h:r0 + n] = (ZB[3, :, r0 + h:r0 + n].astype(F32) + R2[:, s0:s0 + h].astype(F32)).astype(BF)
        send("Z2La" + str(k), ZB.at[3, :, r0 + h:r0 + n], FR.at[:, r0 + h:r0 + n], d_zl)

    outs = []

    def finish(k):
        r0, n = CHUNKS[k]
        h = n // 2
        recv("Z2Rb" + str(k), FL.at[:, r0 + h:r0 + n], d_zl)
        recv("Z2Lb" + str(k), FR.at[:, r0:r0 + h], d_zr)
        recv("Z2Ra" + str(k), FL.at[:, r0:r0 + h], d_zl)
        recv("Z2La" + str(k), FR.at[:, r0 + h:r0 + n], d_zr)
        total = (ZB[0, :, r0:r0 + n].astype(F32) + FL[:, r0:r0 + n].astype(F32) + FR[:, r0:r0 + n].astype(F32)).astype(BF)
        if r0 < 512:
            dgv[:, r0:r0 + n] = total
            copy = pltpu.make_async_copy(dgv.at[:, r0:r0 + n], dg_h.at[:, r0:r0 + n], ls.at[9 + k])
        else:
            ugv[...] = total
            copy = pltpu.make_async_copy(ugv, ug_h, ls.at[9 + k])
        copy.start()
        outs.append(copy)

    def down_term(k):
        def body(b, carry):
            rows = pl.ds(pl.multiple_of(b * 512, 512), 512)
            value = dot(backb[b], xv[rows, 128 * k:128 * k + 128])
            YB[y, b, 128 * k:128 * k + 128, :] = (value.T * (scale_of(b) * norm)).astype(BF)
            return carry
        lax.fori_loop(0, 4, body, 0)

    def input_grad(b):
        ad = scale_of(b)[:, 0:1]

        def body(i, carry):
            rows = pl.ds(pl.multiple_of(i * 128, 128), 128)
            acc = dot(wv[rows, 0:256], features(0, 512 * b, 512))
            for g in range(1, 4):
                acc = acc + dot(wv[rows, 256 * g:256 * g + 256], features(g, 512 * b, 512))
            extra = dot(asel[b, rows, :], backb[b])
            value = acc.astype(BF).astype(F32) + ad * extra
            igv[512 * b:512 * b + 512, rows] = value.T.astype(BF)
            return carry

        lax.fori_loop(0, 4, body, 0)
        copy = pltpu.make_async_copy(igv.at[512 * b:512 * b + 512], ig_h.at[512 * b:512 * b + 512], ls.at[5 + b])
        copy.start()
        outs.append(copy)

    for k in range(4):
        down_term(k)
        y_send(k)

    def up_body(i, carry):
        g, b = i // 4, i % 4
        V[g, b] = dot(features(g, 512 * b, 512), low[b]).astype(BF)
        return carry

    lax.fori_loop(0, 16, up_body, 0)
    send("X1R", V.at[xo, :, 0:128], XR1, d_xr)
    send("X1L", V.at[xo, :, 128:256], XR2, d_xl)
    send("X2Rb", V.at[xr, :, 128:256], XFL.at[:, 128:256], d_xr)
    send("X2Lb", V.at[xl, :, 0:128], XFR.at[:, 0:128], d_xl)

    y_forward(0)
    recv("X1R", XR1, d_xl)
    V[xr, :, 0:128] = (V[xr, :, 0:128].astype(F32) + XR1[...].astype(F32)).astype(BF)
    send("X2Ra", V.at[xr, :, 0:128], XFL.at[:, 0:128], d_xr)
    recv("X1L", XR2, d_xr)
    V[xl, :, 128:256] = (V[xl, :, 128:256].astype(F32) + XR2[...].astype(F32)).astype(BF)
    send("X2La", V.at[xl, :, 128:256], XFR.at[:, 128:256], d_xl)
    combine(0)
    y_forward(1)
    pass_on(0)
    combine(1)
    recv("X2Rb", XFL.at[:, 128:256], d_xl)
    recv("X2Lb", XFR.at[:, 0:128], d_xr)
    recv("X2Ra", XFL.at[:, 0:128], d_xl)
    recv("X2La", XFR.at[:, 128:256], d_xr)
    for s in range(4):
        rows = slice(64 * s, 64 * s + 64)
        XS[s] = (V[x, :, rows].astype(F32) + XFL[:, rows].astype(F32) + XFR[:, rows].astype(F32)).astype(BF)
    me = z * 2 + c
    o1, o2, o3 = (1 - z) * 2 + c, z * 2 + 1 - c, (1 - z) * 2 + 1 - c
    send("Q1", XS.at[o1], QR.at[me], d_z)
    send("Q2", XS.at[o2], QR.at[me], d_c)
    send("Q3", XS.at[o3], QR.at[me], d_zc)
    c_w.wait()
    y_forward(2)
    pass_on(1)
    combine(2)
    recv("Q1", QR.at[o1], d_z)
    recv("Q2", QR.at[o2], d_c)
    recv("Q3", QR.at[o3], d_zc)

    def own_body(b, carry):
        total = XS[me, b].astype(F32) + QR[o1, b].astype(F32) + QR[o2, b].astype(F32) + QR[o3, b].astype(F32)
        YB[y, b, 512:576, :] = (total * (scale_of(b) * norm)).astype(BF)
        return carry

    lax.fori_loop(0, 4, own_body, 0)
    y_send(4)
    y_forward(3)
    pass_on(2)
    combine(3)
    y_forward(4)
    input_grad(0)
    pass_on(3)
    combine(4)
    input_grad(1)
    pass_on(4)
    input_grad(2)
    input_grad(3)
    for k in range(5):
        finish(k)
    for copy in outs:
        copy.wait()
    for copy in sent:
        copy.wait_send()


def per_device(tokens, cotangent, value_weight, adapter_down, adapter_up, pair_ids, ranks):
    rows, width = tokens.shape
    norm = 1.0 / math.sqrt(rows * lax.axis_size("pair"))
    cot = cotangent.T
    up = jnp.swapaxes(adapter_up, 1, 2)
    any_spec = pl.BlockSpec(memory_space=pl.ANY)
    smem = pl.BlockSpec(memory_space=pltpu.SMEM)
    count = len(NAMES)
    vm = pltpu.VMEM
    import functools
    out = pl.pallas_call(
        functools.partial(kernel, norm),
        out_shape=(
            jax.ShapeDtypeStruct((2048, 512), BF),
            jax.ShapeDtypeStruct((3, 512, 128), BF),
            jax.ShapeDtypeStruct((3, 64, 128), BF),
        ),
        in_specs=[smem, smem] + [any_spec] * 5,
        out_specs=(any_spec,) * 3,
        scratch_shapes=[
            vm((4, 2, 2, 64, 2560), BF),
            vm((2048, 512), BF),
            vm((512, 1024), BF),
            vm((48, 512, 128), BF),
            vm((48, 64, 128), BF),
            vm((4, 512, 128), BF),
            vm((4, 512, 128), BF),
            vm((4, 128, 512), F32),
            vm((4, 128, 512), BF),
            vm((4, 4, 576, 128), BF),
            vm((4, 3, 576, 128), BF),
            vm((3, 288, 128), BF),
            vm((3, 288, 128), BF),
            vm((3, 576, 128), BF),
            vm((3, 576, 128), BF),
            vm((4, 4, 256, 128), BF),
            vm((4, 128, 128), BF),
            vm((4, 128, 128), BF),
            vm((4, 256, 128), BF),
            vm((4, 256, 128), BF),
            vm((4, 4, 64, 128), BF),
            vm((4, 4, 64, 128), BF),
            vm((4, 8, 256), jnp.int32),
            vm((192, 256), BF),
            vm((2048, 512), BF),
            vm((3, 512, 128), BF),
            vm((3, 64, 128), BF),
            pltpu.SemaphoreType.DMA((count,)),
            pltpu.SemaphoreType.DMA((count,)),
            pltpu.SemaphoreType.DMA((14,)),
        ],
        compiler_params=pltpu.CompilerParams(
            collective_id=0, has_side_effects=True, vmem_limit_bytes=60 * 1024 * 1024
        ),
    )(pair_ids, ranks, tokens, cot, value_weight, adapter_down, up)
    return out[0], out[1], jnp.swapaxes(out[2], 1, 2)


def solution(mesh):
    placed = (
        P("pair", "fsdp"),
        P("pair", "fsdp"),
        P("fsdp", None),
        P(None, "fsdp", None),
        P(None, None, "fsdp"),
        P("pair"),
        P(),
    )
    return jax.shard_map(
        per_device,
        mesh=mesh,
        in_specs=placed,
        out_specs=(P("pair", "fsdp"), P("pair", "fsdp", None), P("pair", None, "fsdp")),
        check_vma=False,
    )
```

```python
import math

import jax
import jax.numpy as jnp
from jax import lax
from jax.experimental import pallas as pl
from jax.experimental.pallas import tpu as pltpu
from jax.sharding import PartitionSpec as P

MESH = pl.DeviceIdType.MESH
BF = jnp.bfloat16
F32 = jnp.float32

NAMES = ["A1", "B1R", "B1L", "B3O", "A2R", "A2L", "A2RZ", "A2LZ", "B2R", "B2L", "B3L", "B3R", "A3R", "A3L", "A3RZ", "A3LZ", "B3F", "C0", "CL", "CR", "CF"]
NAMES += ["IR", "IL", "IF", "JR", "JL", "JF"]
NAMES += ["X1R", "X1L", "X2Rb", "X2Lb", "X2Ra", "X2La", "Q1", "Q2"]
CHUNKS = [(0, 32), (32, 96), (128, 64), (192, 96), (288, 128), (416, 96), (512, 64)]
SWAPPED = 1
for _k in range(len(CHUNKS)):
    NAMES += [n + str(_k) for n in ("YR", "YL", "YFR", "YFL", "Z1R", "Z1L", "Z2Rb", "Z2Lb", "Z2Ra", "Z2La")]
INDEX = {n: i for i, n in enumerate(NAMES)}


def dot(a, b, ca=1, cb=0):
    return lax.dot_general(a, b, (((ca,), (cb,)), ((), ())), preferred_element_type=F32)


def kernel(norm, ids, ranks, tok_h, cot_h, w_h, a_h, b_h, igv, dgv, ugv,
           G, xv, wv, av, bv, asel, low, backf, backb, YB, ZB, R1, R2, FL, FR,
           V, XR1, XR2, XFL, XFR, XS, QR, idt, jdt, Lm, ss, rs, ls):
    f = lax.axis_index("fsdp")
    q = lax.axis_index("pair")
    x, z, c = f // 4, (f // 2) % 2, f % 2
    zh, y = q // 4, q % 4
    xr, xl, xo = (x + 1) % 4, (x + 3) % 4, (x + 2) % 4
    yr, yl, yo = (y + 1) % 4, (y + 3) % 4, (y + 2) % 4
    zr, zl, zo = (zh + 1) % 4, (zh + 3) % 4, (zh + 2) % 4

    def dev(xx, zz, cc):
        return {"fsdp": xx * 4 + zz * 2 + cc}

    def pdev(zz, yy):
        return {"pair": zz * 4 + yy}

    d_z, d_c = dev(x, 1 - z, c), dev(x, z, 1 - c)
    d_xr, d_xl = dev(xr, z, c), dev(xl, z, c)
    d_yr, d_yl = pdev(zh, yr), pdev(zh, yl)
    d_zr, d_zl = pdev(zr, y), pdev(zl, y)

    plain = ((y, yl, yr, yo), d_yl, d_yr, d_zl, d_zr)
    swapped = ((zh, zl, zr, zo), d_zl, d_zr, d_yl, d_yr)
    role = [swapped if k == SWAPPED else plain for k in range(len(CHUNKS))]

    sent = {}

    def send(name, src, dst, device):
        i = INDEX[name]
        copy = pltpu.make_async_remote_copy(src_ref=src, dst_ref=dst, send_sem=ss.at[i], recv_sem=rs.at[i],
                                            device_id=device, device_id_type=MESH)
        copy.start()
        sent[name] = copy

    def gone(*names):
        for name in names:
            sent.pop(name).wait_send()

    def recv(name, dst, device):
        i = INDEX[name]
        pltpu.make_async_remote_copy(src_ref=dst, dst_ref=dst, send_sem=ss.at[i], recv_sem=rs.at[i],
                                     device_id=device, device_id_type=MESH).wait_recv()

    c_cot = pltpu.make_async_copy(cot_h, G.at[x, z, c, :, 0:2048], ls.at[0])
    c_cot.start()
    c_b = pltpu.make_async_copy(b_h, bv, ls.at[1])
    c_b.start()

    barrier = pltpu.get_barrier_semaphore()
    for device in (d_z, d_c, d_xr, d_xl, d_yr, d_yl, d_zr, d_zl):
        pl.semaphore_signal(barrier, inc=1, device_id=device, device_id_type=MESH)

    lane = lax.broadcasted_iota(jnp.int32, (8, 256), 1)
    part = (lane >> 4) & 3
    tile = jnp.where(part == 0, ids[0], jnp.where(part == 1, ids[1], jnp.where(part == 2, ids[2], ids[3])))
    idt[y] = tile
    jdt[zh] = tile
    c_x = pltpu.make_async_copy(tok_h, xv, ls.at[2])
    c_a = pltpu.make_async_copy(a_h, av, ls.at[3])
    c_w = pltpu.make_async_copy(w_h, wv, ls.at[4])

    L0, L1 = slice(0, 1408), slice(1408, 2560)

    def relay(name, part, device):
        send(name, part, part, device)

    c_cot.wait()
    pl.semaphore_wait(barrier, 8)
    relay("A1", G.at[x, z, c, :, L0], d_z)
    c_b.wait()
    for b in range(4):
        G[x, z, c, :, 2048 + 128 * b:2176 + 128 * b] = bv[ids[b]]
    relay("B1R", G.at[x, z, c, :, L1], d_xr)
    relay("B1L", G.at[x, z, c, :, L1], d_xl)
    relay("B3O", G.at[x, z, c, :, L1], d_z)
    relay("A2R", G.at[x, z, c, :, L0], d_xr)
    relay("A2L", G.at[x, z, c, :, L0], d_xl)
    for copy in (c_x, c_a, c_w):
        copy.start()
    relay("IR", idt.at[y], d_yr)
    relay("IL", idt.at[y], d_yl)
    relay("JR", jdt.at[zh], d_zr)
    relay("JL", jdt.at[zh], d_zl)

    def rank_of(b):
        return ranks[ids[b]]

    def scale_of(b):
        return 32.0 / jnp.broadcast_to(rank_of(b), (1, 128)).astype(F32)

    def features(g, start, count):
        start = pl.multiple_of(start, 128)
        return G[g, :, :, :, pl.ds(start, count)].reshape(256, count)

    def low_all():
        for b in range(4):
            asel[b] = av[ids[b]]

        def body(b, carry):
            value = dot(xv[pl.ds(pl.multiple_of(b * 512, 512), 512), :], asel[b])
            keep = lax.broadcasted_iota(jnp.int32, (512, 128), 1) < rank_of(b)
            low[b] = jnp.where(keep, value, 0.0).astype(BF)
            return carry

        lax.fori_loop(0, 4, body, 0)

    def back_step(g, first):
        for b in range(4):
            value = dot(features(g, 2048 + 128 * b, 128), features(g, 512 * b, 512), 0, 0)
            if first:
                backf[b] = value
            else:
                backf[b] = backf[b] + value

    def back_last(g):
        for b in range(4):
            value = backf[b] + dot(features(g, 2048 + 128 * b, 128), features(g, 512 * b, 512), 0, 0)
            keep = lax.broadcasted_iota(jnp.int32, (128, 512), 0) < rank_of(b)
            backb[b] = jnp.where(keep, value, 0.0).astype(BF)

    def up_step(g):
        def body(b, carry):
            V[g, b] = dot(features(g, 512 * b, 512), low[b]).astype(BF)
            return carry
        lax.fori_loop(0, 4, body, 0)

    def onehot(which):
        row = lax.broadcasted_iota(jnp.int32, (192, 256), 0)
        col = lax.broadcasted_iota(jnp.int32, (192, 256), 1)
        slot = row >> 4
        turn = (slot >= 3).astype(jnp.int32) + (slot >= 6).astype(jnp.int32) + (slot >= 9).astype(jnp.int32)
        if which:
            owner = zh * 4 + ((y + turn) & 3)
        else:
            owner = ((zh + turn) & 3) * 4 + y
        pair = 3 * owner + slot - 3 * turn
        of_block = jnp.zeros((192, 256), jnp.int32)
        table = jdt if which else idt
        for s in range(4):
            of_block = jnp.where((col >> 6) == s, jnp.broadcast_to(table[s][0:1, :], (192, 256)), of_block)
        hit = jnp.logical_and((row & 15) == (col & 15), of_block == pair)
        Lm[which] = jnp.where(hit, 1.0, 0.0).astype(BF)

    def y_send(k):
        r0, n = CHUNKS[k]
        (me, _, _, _), al, ar, _, _ = role[k]
        own = YB.at[me, :, r0:r0 + n]
        relay("YR" + str(k), own, ar)
        relay("YL" + str(k), own, al)

    def y_forward(k):
        r0, n = CHUNKS[k]
        h = n // 2
        (_, il, ir, _), al, ar, _, _ = role[k]
        recv("YR" + str(k), YB.at[il, :, r0:r0 + n], al)
        relay("YFR" + str(k), YB.at[il, :, r0:r0 + h], ar)
        recv("YL" + str(k), YB.at[ir, :, r0:r0 + n], ar)
        relay("YFL" + str(k), YB.at[ir, :, r0 + h:r0 + n], al)

    def combine_math(k):
        r0, n = CHUNKS[k]
        which = 1 if k == SWAPPED else 0

        def body(i, carry):
            top = pl.ds(pl.multiple_of(r0 + 32 * i, 16), 16)
            bottom = pl.ds(pl.multiple_of(r0 + 32 * i + 16, 16), 16)
            stack = jnp.concatenate([YB[:, :, top, :].reshape(256, 128), YB[:, :, bottom, :].reshape(256, 128)], axis=1)
            out = dot(Lm[which], stack).astype(BF)
            ZB[:, :, top, :] = out[:, 0:128].reshape(4, 3, 16, 128)
            ZB[:, :, bottom, :] = out[:, 128:256].reshape(4, 3, 16, 128)
            return carry

        lax.fori_loop(0, n // 32, body, 0)

    def combine(k):
        r0, n = CHUNKS[k]
        h = n // 2
        s0 = r0 // 2
        (_, _, _, io), al, ar, bl, br = role[k]
        recv("YFR" + str(k), YB.at[io, :, r0:r0 + h], al)
        recv("YFL" + str(k), YB.at[io, :, r0 + h:r0 + n], ar)
        combine_math(k)
        send("Z1R" + str(k), ZB.at[2, :, r0:r0 + h], R1.at[:, s0:s0 + h], br)
        send("Z1L" + str(k), ZB.at[2, :, r0 + h:r0 + n], R2.at[:, s0:s0 + h], bl)

    def z_rest(k):
        r0, n = CHUNKS[k]
        h = n // 2
        _, _, _, bl, br = role[k]
        send("Z2Rb" + str(k), ZB.at[1, :, r0 + h:r0 + n], FL.at[:, r0 + h:r0 + n], br)
        send("Z2Lb" + str(k), ZB.at[3, :, r0:r0 + h], FR.at[:, r0:r0 + h], bl)

    def pass_on(k):
        r0, n = CHUNKS[k]
        h = n // 2
        s0 = r0 // 2
        _, _, _, bl, br = role[k]
        recv("Z1R" + str(k), R1.at[:, s0:s0 + h], bl)
        ZB[1, :, r0:r0 + h] = (ZB[1, :, r0:r0 + h].astype(F32) + R1[:, s0:s0 + h].astype(F32)).astype(BF)
        send("Z2Ra" + str(k), ZB.at[1, :, r0:r0 + h], FL.at[:, r0:r0 + h], br)
        recv("Z1L" + str(k), R2.at[:, s0:s0 + h], br)
        ZB[3, :, r0 + h:r0 + n] = (ZB[3, :, r0 + h:r0 + n].astype(F32) + R2[:, s0:s0 + h].astype(F32)).astype(BF)
        send("Z2La" + str(k), ZB.at[3, :, r0 + h:r0 + n], FR.at[:, r0 + h:r0 + n], bl)

    def finish(k):
        r0, n = CHUNKS[k]
        h = n // 2
        _, _, _, bl, br = role[k]
        recv("Z2Rb" + str(k), FL.at[:, r0 + h:r0 + n], bl)
        recv("Z2Lb" + str(k), FR.at[:, r0:r0 + h], br)
        recv("Z2Ra" + str(k), FL.at[:, r0:r0 + h], bl)
        recv("Z2La" + str(k), FR.at[:, r0 + h:r0 + n], br)
        total = (ZB[0, :, r0:r0 + n].astype(F32) + FL[:, r0:r0 + n].astype(F32) + FR[:, r0:r0 + n].astype(F32)).astype(BF)
        if r0 < 512:
            dgv[:, r0:r0 + n] = total
        else:
            ugv[...] = total

    def down_term(k):
        for b in range(4):
            value = dot(backb[b], xv[512 * b:512 * b + 512, 128 * k:128 * k + 128])
            value = (value.T * (scale_of(b) * norm)).astype(BF)
            if k == 0:
                YB[y, b, 0:32, :] = value[0:32]
                YB[zh, b, 32:128, :] = value[32:128]
            else:
                YB[y, b, 128 * k:128 * k + 128, :] = value

    def input_grad(b):
        ad = scale_of(b)[:, 0:1]

        def body(i, carry):
            rows = pl.ds(pl.multiple_of(i * 128, 128), 128)
            acc = dot(wv[rows, 0:256], features(0, 512 * b, 512))
            for g in range(1, 4):
                acc = acc + dot(wv[rows, 256 * g:256 * g + 256], features(g, 512 * b, 512))
            extra = dot(asel[b, rows, :], backb[b])
            value = acc.astype(BF).astype(F32) + ad * extra
            igv[512 * b:512 * b + 512, rows] = value.T.astype(BF)
            return carry

        lax.fori_loop(0, 4, body, 0)

    c_a.wait()
    c_x.wait()
    low_all()
    recv("B1R", G.at[xl, z, c, :, L1], d_xl)
    relay("B2R", G.at[xl, z, c, 0:32, L1], d_xr)
    relay("B3L", G.at[xl, z, c, :, L1], d_z)
    recv("B1L", G.at[xr, z, c, :, L1], d_xr)
    relay("B2L", G.at[xr, z, c, 32:64, L1], d_xl)
    relay("B3R", G.at[xr, z, c, :, L1], d_z)
    recv("A1", G.at[x, 1 - z, c, :, L0], d_z)
    relay("A2RZ", G.at[x, 1 - z, c, :, L0], d_xr)
    relay("A2LZ", G.at[x, 1 - z, c, :, L0], d_xl)
    recv("IR", idt.at[yl], d_yl)
    relay("IF", idt.at[yl], d_yr)
    recv("B3O", G.at[x, 1 - z, c, :, L1], d_z)
    relay("C0", G.at[x, :, c], d_c)
    recv("A2R", G.at[xl, z, c, :, L0], d_xl)
    relay("A3R", G.at[xl, z, c, 0:32, L0], d_xr)
    recv("A2L", G.at[xr, z, c, :, L0], d_xr)
    relay("A3L", G.at[xr, z, c, 32:64, L0], d_xl)
    recv("B2R", G.at[xo, z, c, 0:32, L1], d_xl)
    recv("B2L", G.at[xo, z, c, 32:64, L1], d_xr)
    relay("B3F", G.at[xo, z, c, :, L1], d_z)
    recv("C0", G.at[x, :, 1 - c], d_c)
    back_step(x, True)
    up_step(x)
    recv("IL", idt.at[yr], d_yr)
    recv("IF", idt.at[yo], d_yl)
    onehot(0)
    recv("A2RZ", G.at[xl, 1 - z, c, :, L0], d_xl)
    relay("A3RZ", G.at[xl, 1 - z, c, 0:32, L0], d_xr)
    recv("A2LZ", G.at[xr, 1 - z, c, :, L0], d_xr)
    relay("A3LZ", G.at[xr, 1 - z, c, 32:64, L0], d_xl)
    recv("B3L", G.at[xl, 1 - z, c, :, L1], d_z)
    relay("CL", G.at[xl, :, c], d_c)
    recv("B3R", G.at[xr, 1 - z, c, :, L1], d_z)
    relay("CR", G.at[xr, :, c], d_c)
    recv("CL", G.at[xl, :, 1 - c], d_c)
    back_step(xl, False)
    up_step(xl)
    recv("CR", G.at[xr, :, 1 - c], d_c)
    back_step(xr, False)
    recv("A3R", G.at[xo, z, c, 0:32, L0], d_xl)
    recv("A3L", G.at[xo, z, c, 32:64, L0], d_xr)
    recv("A3RZ", G.at[xo, 1 - z, c, 0:32, L0], d_xl)
    recv("A3LZ", G.at[xo, 1 - z, c, 32:64, L0], d_xr)
    recv("B3F", G.at[xo, 1 - z, c, :, L1], d_z)
    relay("CF", G.at[xo, :, c], d_c)
    recv("JR", jdt.at[zl], d_zl)
    relay("JF", jdt.at[zl], d_zr)
    up_step(xr)
    recv("CF", G.at[xo, :, 1 - c], d_c)
    back_last(xo)

    down_term(0)
    y_send(0)
    y_send(1)
    down_term(1)
    y_send(2)
    down_term(2)
    up_step(xo)
    send("X1R", V.at[xo, :, 0:128], XR1, d_xr)
    send("X1L", V.at[xo, :, 128:256], XR2, d_xl)
    send("X2Rb", V.at[xr, :, 128:256], XFL.at[:, 128:256], d_xr)
    send("X2Lb", V.at[xl, :, 0:128], XFR.at[:, 0:128], d_xl)
    y_forward(0)
    y_send(3)
    down_term(3)
    y_forward(2)
    y_send(4)
    combine(0)
    z_rest(0)
    recv("X1R", XR1, d_xl)
    V[xr, :, 0:128] = (V[xr, :, 0:128].astype(F32) + XR1[...].astype(F32)).astype(BF)
    send("X2Ra", V.at[xr, :, 0:128], XFL.at[:, 0:128], d_xr)
    recv("X1L", XR2, d_xr)
    V[xl, :, 128:256] = (V[xl, :, 128:256].astype(F32) + XR2[...].astype(F32)).astype(BF)
    send("X2La", V.at[xl, :, 128:256], XFR.at[:, 128:256], d_xl)
    y_forward(3)
    y_send(5)
    y_forward(1)
    combine(2)
    z_rest(2)
    pass_on(0)
    y_forward(4)
    combine(3)
    z_rest(3)
    recv("JL", jdt.at[zr], d_zr)
    recv("JF", jdt.at[zo], d_zl)
    onehot(1)
    pass_on(2)
    recv("X2Rb", XFL.at[:, 128:256], d_xl)
    recv("X2Lb", XFR.at[:, 0:128], d_xr)
    recv("X2Ra", XFL.at[:, 0:128], d_xl)
    recv("X2La", XFR.at[:, 128:256], d_xr)
    for s in range(4):
        rows = slice(64 * s, 64 * s + 64)
        XS[s % 2, s // 2] = (V[x, :, rows].astype(F32) + XFL[:, rows].astype(F32) + XFR[:, rows].astype(F32)).astype(BF)
    send("Q2", XS.at[1 - c], QR.at[0:2], d_c)
    y_forward(5)
    combine(1)
    z_rest(1)
    recv("Q2", QR.at[0:2], d_c)
    XS[c, 1 - z] = (XS[c, 1 - z].astype(F32) + QR[1 - z].astype(F32)).astype(BF)
    send("Q1", XS.at[c, 1 - z], QR.at[2], d_z)
    combine(4)
    pass_on(3)
    z_rest(4)
    pass_on(1)
    combine(5)
    c_w.wait()
    input_grad(0)
    input_grad(1)
    recv("Q1", QR.at[2], d_z)

    def own_body(b, carry):
        total = XS[c, z, b].astype(F32) + QR[z, b].astype(F32) + QR[2, b].astype(F32)
        YB[y, b, 512:576, :] = (total * (scale_of(b) * norm)).astype(BF)
        return carry

    lax.fori_loop(0, 4, own_body, 0)
    y_send(6)
    pass_on(4)
    y_forward(6)
    finish(0)
    finish(1)
    finish(2)
    input_grad(2)
    combine(6)
    z_rest(5)
    pass_on(5)
    z_rest(6)
    finish(3)
    input_grad(3)
    pass_on(6)
    for k in (4, 5, 6):
        finish(k)
    gone(*list(sent))


def drain(ig, dg, ug, ig_h, dg_h, ug_h, sem):
    copies = [pltpu.make_async_copy(src, dst, sem.at[i]) for i, (src, dst) in enumerate(((ig, ig_h), (dg, dg_h), (ug, ug_h)))]
    for copy in copies:
        copy.start()
    for copy in copies:
        copy.wait()


def per_device(tokens, cotangent, value_weight, adapter_down, adapter_up, pair_ids, ranks):
    rows, width = tokens.shape
    norm = 1.0 / math.sqrt(rows * lax.axis_size("pair"))
    cot = cotangent.T
    up = jnp.swapaxes(adapter_up, 1, 2)
    any_spec = pl.BlockSpec(memory_space=pltpu.HBM)
    smem = pl.BlockSpec(memory_space=pltpu.SMEM)
    count = len(NAMES)
    vm = pltpu.VMEM
    import functools
    out = pl.pallas_call(
        functools.partial(kernel, norm),
        out_shape=(
            vm((2048, 512), BF),
            vm((3, 512, 128), BF),
            vm((3, 64, 128), BF),
        ),
        in_specs=[smem, smem] + [any_spec] * 5,
        out_specs=(pl.BlockSpec(memory_space=pltpu.VMEM),) * 3,
        scratch_shapes=[
            vm((4, 2, 2, 64, 2560), BF),
            vm((2048, 512), BF),
            vm((512, 1024), BF),
            vm((48, 512, 128), BF),
            vm((48, 64, 128), BF),
            vm((4, 512, 128), BF),
            vm((4, 512, 128), BF),
            vm((4, 128, 512), F32),
            vm((4, 128, 512), BF),
            vm((4, 4, 576, 128), BF),
            vm((4, 3, 576, 128), BF),
            vm((3, 288, 128), BF),
            vm((3, 288, 128), BF),
            vm((3, 576, 128), BF),
            vm((3, 576, 128), BF),
            vm((4, 4, 256, 128), BF),
            vm((4, 128, 128), BF),
            vm((4, 128, 128), BF),
            vm((4, 256, 128), BF),
            vm((4, 256, 128), BF),
            vm((2, 2, 4, 64, 128), BF),
            vm((3, 4, 64, 128), BF),
            vm((4, 8, 256), jnp.int32),
            vm((4, 8, 256), jnp.int32),
            vm((2, 192, 256), BF),
            pltpu.SemaphoreType.DMA((count,)),
            pltpu.SemaphoreType.DMA((count,)),
            pltpu.SemaphoreType.DMA((5,)),
        ],
        compiler_params=pltpu.CompilerParams(
            collective_id=0, has_side_effects=True, vmem_limit_bytes=60 * 1024 * 1024
        ),
    )(pair_ids, ranks, tokens, cot, value_weight, adapter_down, up)
    out = [pltpu.with_memory_space_constraint(part, pltpu.VMEM) for part in out]
    out = pl.pallas_call(
        drain,
        out_shape=tuple(jax.ShapeDtypeStruct(part.shape, BF) for part in out),
        in_specs=[pl.BlockSpec(memory_space=pltpu.VMEM)] * 3,
        out_specs=(any_spec,) * 3,
        scratch_shapes=[pltpu.SemaphoreType.DMA((3,))],
        compiler_params=pltpu.CompilerParams(vmem_limit_bytes=1024 * 1024),
    )(*out)
    return out[0], out[1], jnp.swapaxes(out[2], 1, 2)


def solution(mesh):
    placed = (
        P("pair", "fsdp"),
        P("pair", "fsdp"),
        P("fsdp", None),
        P(None, "fsdp", None),
        P(None, None, "fsdp"),
        P("pair"),
        P(),
    )
    return jax.shard_map(
        per_device,
        mesh=mesh,
        in_specs=placed,
        out_specs=(P("pair", "fsdp"), P("pair", "fsdp", None), P("pair", None, "fsdp")),
        check_vma=False,
    )
```

```python
import math

import jax
import jax.numpy as jnp
from jax import lax
from jax.experimental import pallas as pl
from jax.experimental.pallas import tpu as pltpu
from jax.sharding import PartitionSpec as P

MESH = pl.DeviceIdType.MESH
BF = jnp.bfloat16
F32 = jnp.float32

NAMES = ["A1", "B1R", "B1L", "B3O", "A2R", "A2L", "A2RZ", "A2LZ", "B2R", "B2L", "B3L", "B3R", "A3R", "A3L", "A3RZ", "A3LZ", "B3F", "C0", "CL", "CR", "CE", "CF"]
NAMES += ["IR", "IL", "IF", "JR", "JL", "JF"]
NAMES += ["X1R", "X1L", "X2Rb", "X2Lb", "X2Ra", "X2La", "Q1", "Q2"]
CHUNKS = [(0, 32), (32, 160), (192, 64), (256, 96), (352, 96), (448, 64), (512, 64)]
SWAPPED = 1
for _k in range(len(CHUNKS)):
    NAMES += [n + str(_k) for n in ("YR", "YL", "YFR", "YFL", "Z1R", "Z1L", "Z2Rb", "Z2Lb", "Z2Ra", "Z2La")]
INDEX = {n: i for i, n in enumerate(NAMES)}


def dot(a, b, ca=1, cb=0):
    return lax.dot_general(a, b, (((ca,), (cb,)), ((), ())), preferred_element_type=F32)


def kernel(norm, ids_h, ranks_h, tok_h, cot_h, w_h, a_h, b_h, igv, dgv, ugv,
           G, xv, wv, av, bv, asel, low, backf, backb, YB, ZB, R1, R2, FL, FR,
           V, XR1, XR2, XFL, XFR, XS, QR, idt, jdt, Lm, ids, ranks, ss, rs, ls):
    f = lax.axis_index("fsdp")
    q = lax.axis_index("pair")
    x, z, c = f // 4, (f // 2) % 2, f % 2
    zh, y = q // 4, q % 4
    xr, xl, xo = (x + 1) % 4, (x + 3) % 4, (x + 2) % 4
    yr, yl, yo = (y + 1) % 4, (y + 3) % 4, (y + 2) % 4
    zr, zl, zo = (zh + 1) % 4, (zh + 3) % 4, (zh + 2) % 4

    def dev(xx, zz, cc):
        return {"fsdp": xx * 4 + zz * 2 + cc}

    def pdev(zz, yy):
        return {"pair": zz * 4 + yy}

    d_z, d_c = dev(x, 1 - z, c), dev(x, z, 1 - c)
    d_xr, d_xl = dev(xr, z, c), dev(xl, z, c)
    d_yr, d_yl = pdev(zh, yr), pdev(zh, yl)
    d_zr, d_zl = pdev(zr, y), pdev(zl, y)

    plain = ((y, yl, yr, yo), d_yl, d_yr, d_zl, d_zr)
    swapped = ((zh, zl, zr, zo), d_zl, d_zr, d_yl, d_yr)
    role = [swapped if k == SWAPPED else plain for k in range(len(CHUNKS))]

    sent = {}

    def send(name, src, dst, device):
        i = INDEX[name]
        copy = pltpu.make_async_remote_copy(src_ref=src, dst_ref=dst, send_sem=ss.at[i], recv_sem=rs.at[i],
                                            device_id=device, device_id_type=MESH)
        copy.start()
        sent[name] = copy

    def gone(*names):
        for name in names:
            sent.pop(name).wait_send()

    def recv(name, dst, device):
        i = INDEX[name]
        pltpu.make_async_remote_copy(src_ref=dst, dst_ref=dst, send_sem=ss.at[i], recv_sem=rs.at[i],
                                     device_id=device, device_id_type=MESH).wait_recv()

    c_cot = pltpu.make_async_copy(cot_h, G.at[x, z, c, :, 0:2048], ls.at[0])
    c_ids = pltpu.make_async_copy(ids_h, ids, ls.at[5])
    c_b = pltpu.make_async_copy(b_h, bv, ls.at[1])
    c_ranks = pltpu.make_async_copy(ranks_h, ranks, ls.at[6])
    for copy in (c_cot, c_ids, c_b, c_ranks):
        copy.start()

    barrier = pltpu.get_barrier_semaphore()
    for device in (d_z, d_c, d_xr, d_xl, d_yr, d_yl, d_zr, d_zl):
        pl.semaphore_signal(barrier, inc=1, device_id=device, device_id_type=MESH)

    c_x = pltpu.make_async_copy(tok_h, xv, ls.at[2])
    c_a = pltpu.make_async_copy(a_h, av, ls.at[3])
    c_w = pltpu.make_async_copy(w_h, wv, ls.at[4])

    L0, L1 = slice(0, 1408), slice(1408, 2560)

    def relay(name, part, device):
        send(name, part, part, device)

    c_cot.wait()
    pl.semaphore_wait(barrier, 8)
    relay("A1", G.at[x, z, c, :, L0], d_z)
    c_b.wait()
    c_ids.wait()
    c_ranks.wait()
    for b in range(4):
        G[x, z, c, :, 2048 + 128 * b:2176 + 128 * b] = bv[ids[b]]
    relay("B1R", G.at[x, z, c, :, L1], d_xr)
    relay("B1L", G.at[x, z, c, :, L1], d_xl)
    relay("B3O", G.at[x, z, c, :, L1], d_z)
    relay("A2R", G.at[x, z, c, :, L0], d_xr)
    relay("A2L", G.at[x, z, c, :, L0], d_xl)
    for copy in (c_x, c_a, c_w):
        copy.start()
    lane = lax.broadcasted_iota(jnp.int32, (8, 256), 1)
    part = (lane >> 4) & 3
    tile = jnp.where(part == 0, ids[0], jnp.where(part == 1, ids[1], jnp.where(part == 2, ids[2], ids[3])))
    idt[y] = tile
    jdt[zh] = tile
    relay("IR", idt.at[y], d_yr)
    relay("IL", idt.at[y], d_yl)
    relay("JR", jdt.at[zh], d_zr)
    relay("JL", jdt.at[zh], d_zl)

    def rank_of(b):
        return ranks[ids[b]]

    def scale_of(b):
        return 32.0 / jnp.broadcast_to(rank_of(b), (1, 128)).astype(F32)

    def features(g, start, count):
        start = pl.multiple_of(start, 128)
        return G[g, :, :, :, pl.ds(start, count)].reshape(256, count)

    def low_all():
        for b in range(4):
            asel[b] = av[ids[b]]

        def body(b, carry):
            value = dot(xv[pl.ds(pl.multiple_of(b * 512, 512), 512), :], asel[b])
            keep = lax.broadcasted_iota(jnp.int32, (512, 128), 1) < rank_of(b)
            low[b] = jnp.where(keep, value, 0.0).astype(BF)
            return carry

        lax.fori_loop(0, 4, body, 0)

    def back_step(g, first):
        for b in range(4):
            value = dot(features(g, 2048 + 128 * b, 128), features(g, 512 * b, 512), 0, 0)
            if first:
                backf[b] = value
            else:
                backf[b] = backf[b] + value

    def back_last(g):
        for b in range(4):
            value = backf[b] + dot(features(g, 2048 + 128 * b, 128), features(g, 512 * b, 512), 0, 0)
            keep = lax.broadcasted_iota(jnp.int32, (128, 512), 0) < rank_of(b)
            backb[b] = jnp.where(keep, value, 0.0).astype(BF)

    def up_step(g):
        def body(b, carry):
            V[g, b] = dot(features(g, 512 * b, 512), low[b]).astype(BF)
            return carry
        lax.fori_loop(0, 4, body, 0)

    def onehot(which):
        row = lax.broadcasted_iota(jnp.int32, (192, 256), 0)
        col = lax.broadcasted_iota(jnp.int32, (192, 256), 1)
        slot = row >> 4
        turn = (slot >= 3).astype(jnp.int32) + (slot >= 6).astype(jnp.int32) + (slot >= 9).astype(jnp.int32)
        if which:
            owner = zh * 4 + ((y + turn) & 3)
        else:
            owner = ((zh + turn) & 3) * 4 + y
        pair = 3 * owner + slot - 3 * turn
        of_block = jnp.zeros((192, 256), jnp.int32)
        table = jdt if which else idt
        for s in range(4):
            of_block = jnp.where((col >> 6) == s, jnp.broadcast_to(table[s][0:1, :], (192, 256)), of_block)
        hit = jnp.logical_and((row & 15) == (col & 15), of_block == pair)
        Lm[which] = jnp.where(hit, 1.0, 0.0).astype(BF)

    def y_send(k):
        r0, n = CHUNKS[k]
        (me, _, _, _), al, ar, _, _ = role[k]
        own = YB.at[me, :, r0:r0 + n]
        relay("YR" + str(k), own, ar)
        relay("YL" + str(k), own, al)

    def y_forward(k):
        r0, n = CHUNKS[k]
        h = n // 2
        (_, il, ir, _), al, ar, _, _ = role[k]
        recv("YR" + str(k), YB.at[il, :, r0:r0 + n], al)
        relay("YFR" + str(k), YB.at[il, :, r0:r0 + h], ar)
        recv("YL" + str(k), YB.at[ir, :, r0:r0 + n], ar)
        relay("YFL" + str(k), YB.at[ir, :, r0 + h:r0 + n], al)

    def combine_math(k):
        r0, n = CHUNKS[k]
        which = 1 if k == SWAPPED else 0

        def body(i, carry):
            top = pl.ds(pl.multiple_of(r0 + 32 * i, 16), 16)
            bottom = pl.ds(pl.multiple_of(r0 + 32 * i + 16, 16), 16)
            stack = jnp.concatenate([YB[:, :, top, :].reshape(256, 128), YB[:, :, bottom, :].reshape(256, 128)], axis=1)
            out = dot(Lm[which], stack).astype(BF)
            ZB[:, :, top, :] = out[:, 0:128].reshape(4, 3, 16, 128)
            ZB[:, :, bottom, :] = out[:, 128:256].reshape(4, 3, 16, 128)
            return carry

        lax.fori_loop(0, n // 32, body, 0)

    def combine(k):
        r0, n = CHUNKS[k]
        h = n // 2
        s0 = r0 // 2
        (_, _, _, io), al, ar, bl, br = role[k]
        recv("YFR" + str(k), YB.at[io, :, r0:r0 + h], al)
        recv("YFL" + str(k), YB.at[io, :, r0 + h:r0 + n], ar)
        combine_math(k)
        send("Z1R" + str(k), ZB.at[2, :, r0:r0 + h], R1.at[:, s0:s0 + h], br)
        send("Z1L" + str(k), ZB.at[2, :, r0 + h:r0 + n], R2.at[:, s0:s0 + h], bl)

    def z_rest(k):
        r0, n = CHUNKS[k]
        h = n // 2
        _, _, _, bl, br = role[k]
        send("Z2Rb" + str(k), ZB.at[1, :, r0 + h:r0 + n], FL.at[:, r0 + h:r0 + n], br)
        send("Z2Lb" + str(k), ZB.at[3, :, r0:r0 + h], FR.at[:, r0:r0 + h], bl)

    def pass_on(k):
        r0, n = CHUNKS[k]
        h = n // 2
        s0 = r0 // 2
        _, _, _, bl, br = role[k]
        recv("Z1R" + str(k), R1.at[:, s0:s0 + h], bl)
        ZB[1, :, r0:r0 + h] = (ZB[1, :, r0:r0 + h].astype(F32) + R1[:, s0:s0 + h].astype(F32)).astype(BF)
        send("Z2Ra" + str(k), ZB.at[1, :, r0:r0 + h], FL.at[:, r0:r0 + h], br)
        recv("Z1L" + str(k), R2.at[:, s0:s0 + h], br)
        ZB[3, :, r0 + h:r0 + n] = (ZB[3, :, r0 + h:r0 + n].astype(F32) + R2[:, s0:s0 + h].astype(F32)).astype(BF)
        send("Z2La" + str(k), ZB.at[3, :, r0 + h:r0 + n], FR.at[:, r0 + h:r0 + n], bl)

    def finish(k):
        r0, n = CHUNKS[k]
        h = n // 2
        _, _, _, bl, br = role[k]
        recv("Z2Rb" + str(k), FL.at[:, r0 + h:r0 + n], bl)
        recv("Z2Lb" + str(k), FR.at[:, r0:r0 + h], br)
        recv("Z2Ra" + str(k), FL.at[:, r0:r0 + h], bl)
        recv("Z2La" + str(k), FR.at[:, r0 + h:r0 + n], br)
        total = (ZB[0, :, r0:r0 + n].astype(F32) + FL[:, r0:r0 + n].astype(F32) + FR[:, r0:r0 + n].astype(F32)).astype(BF)
        if r0 < 512:
            dgv[:, r0:r0 + n] = total
        else:
            ugv[...] = total

    def down_term(k):
        for b in range(4):
            value = dot(backb[b], xv[512 * b:512 * b + 512, 128 * k:128 * k + 128])
            value = (value.T * (scale_of(b) * norm)).astype(BF)
            for i, (r0, n) in enumerate(CHUNKS):
                lo, hi = max(r0, 128 * k), min(r0 + n, 128 * k + 128)
                if lo < hi:
                    YB[role[i][0][0], b, lo:hi, :] = value[lo - 128 * k:hi - 128 * k]

    def input_grad(b):
        ad = scale_of(b)[:, 0:1]

        def body(i, carry):
            rows = pl.ds(pl.multiple_of(i * 128, 128), 128)
            acc = dot(wv[rows, 0:256], features(0, 512 * b, 512))
            for g in range(1, 4):
                acc = acc + dot(wv[rows, 256 * g:256 * g + 256], features(g, 512 * b, 512))
            extra = dot(asel[b, rows, :], backb[b])
            value = acc.astype(BF).astype(F32) + ad * extra
            igv[512 * b:512 * b + 512, rows] = value.T.astype(BF)
            return carry

        lax.fori_loop(0, 4, body, 0)

    me, other = c, 1 - c

    def up_exchange():
        up_step(xo)
        send("X1R", V.at[xo, :, 0:128], XR1, d_xr)
        send("X1L", V.at[xo, :, 128:256], XR2, d_xl)

    def up_direct():
        send("X2Rb", V.at[xr, :, 128:256], XFL.at[:, 128:256], d_xr)
        send("X2Lb", V.at[xl, :, 0:128], XFR.at[:, 0:128], d_xl)

    def up_pass():
        recv("X1R", XR1, d_xl)
        V[xr, :, 0:128] = (V[xr, :, 0:128].astype(F32) + XR1[...].astype(F32)).astype(BF)
        send("X2Ra", V.at[xr, :, 0:128], XFL.at[:, 0:128], d_xr)
        recv("X1L", XR2, d_xr)
        V[xl, :, 128:256] = (V[xl, :, 128:256].astype(F32) + XR2[...].astype(F32)).astype(BF)
        send("X2La", V.at[xl, :, 128:256], XFR.at[:, 128:256], d_xl)

    def up_split():
        recv("X2Rb", XFL.at[:, 128:256], d_xl)
        recv("X2Lb", XFR.at[:, 0:128], d_xr)
        recv("X2Ra", XFL.at[:, 0:128], d_xl)
        recv("X2La", XFR.at[:, 128:256], d_xr)
        for s in range(4):
            rows = slice(64 * s, 64 * s + 64)
            total = V[x, :, rows].astype(F32) + XFL[:, rows].astype(F32) + XFR[:, rows].astype(F32)
            XS[s % 2, s // 2] = total.astype(BF)
        send("Q2", XS.at[other], QR.at[0:2], d_c)

    def up_cross():
        recv("Q2", QR.at[0:2], d_c)
        XS[me, 1 - z] = (XS[me, 1 - z].astype(F32) + QR[1 - z].astype(F32)).astype(BF)
        send("Q1", XS.at[me, 1 - z], QR.at[2], d_z)

    def up_own():
        recv("Q1", QR.at[2], d_z)

        def body(b, carry):
            total = XS[me, z, b].astype(F32) + QR[z, b].astype(F32) + QR[2, b].astype(F32)
            YB[y, b, 512:576, :] = (total * (scale_of(b) * norm)).astype(BF)
            return carry

        lax.fori_loop(0, 4, body, 0)

    def column_onehot():
        recv("JL", jdt.at[zr], d_zr)
        recv("JF", jdt.at[zo], d_zl)
        onehot(1)

    c_a.wait()
    c_x.wait()
    low_all()
    recv("B1R", G.at[xl, z, c, :, L1], d_xl)
    relay("B2R", G.at[xl, z, c, 0:32, L1], d_xr)
    relay("B3L", G.at[xl, z, c, :, L1], d_z)
    recv("B1L", G.at[xr, z, c, :, L1], d_xr)
    relay("B2L", G.at[xr, z, c, 32:64, L1], d_xl)
    relay("B3R", G.at[xr, z, c, :, L1], d_z)
    recv("A1", G.at[x, 1 - z, c, :, L0], d_z)
    relay("A2RZ", G.at[x, 1 - z, c, :, L0], d_xr)
    relay("A2LZ", G.at[x, 1 - z, c, :, L0], d_xl)
    recv("IR", idt.at[yl], d_yl)
    relay("IF", idt.at[yl], d_yr)
    recv("B3O", G.at[x, 1 - z, c, :, L1], d_z)
    relay("C0", G.at[x, :, c], d_c)
    recv("A2R", G.at[xl, z, c, :, L0], d_xl)
    relay("A3R", G.at[xl, z, c, 0:32, L0], d_xr)
    recv("A2L", G.at[xr, z, c, :, L0], d_xr)
    relay("A3L", G.at[xr, z, c, 32:64, L0], d_xl)
    recv("B2R", G.at[xo, z, c, 0:32, L1], d_xl)
    recv("B2L", G.at[xo, z, c, 32:64, L1], d_xr)
    relay("B3F", G.at[xo, z, c, :, L1], d_z)
    recv("C0", G.at[x, :, 1 - c], d_c)
    back_step(x, True)
    up_step(x)
    recv("IL", idt.at[yr], d_yr)
    recv("IF", idt.at[yo], d_yl)
    onehot(0)
    recv("A2RZ", G.at[xl, 1 - z, c, :, L0], d_xl)
    relay("A3RZ", G.at[xl, 1 - z, c, 0:32, L0], d_xr)
    recv("A2LZ", G.at[xr, 1 - z, c, :, L0], d_xr)
    relay("A3LZ", G.at[xr, 1 - z, c, 32:64, L0], d_xl)
    recv("B3L", G.at[xl, 1 - z, c, :, L1], d_z)
    relay("CL", G.at[xl, :, c], d_c)
    recv("B3R", G.at[xr, 1 - z, c, :, L1], d_z)
    relay("CR", G.at[xr, :, c], d_c)
    recv("A3R", G.at[xo, z, c, 0:32, L0], d_xl)
    recv("A3L", G.at[xo, z, c, 32:64, L0], d_xr)
    relay("CE", G.at[xo, z, c], d_c)
    recv("JR", jdt.at[zl], d_zl)
    relay("JF", jdt.at[zl], d_zr)
    recv("CL", G.at[xl, :, 1 - c], d_c)
    back_step(xl, False)
    recv("A3RZ", G.at[xo, 1 - z, c, 0:32, L0], d_xl)
    recv("A3LZ", G.at[xo, 1 - z, c, 32:64, L0], d_xr)
    recv("B3F", G.at[xo, 1 - z, c, :, L1], d_z)
    relay("CF", G.at[xo, 1 - z, c], d_c)
    recv("CR", G.at[xr, :, 1 - c], d_c)
    back_step(xr, False)
    recv("CE", G.at[xo, z, 1 - c], d_c)
    recv("CF", G.at[xo, 1 - z, 1 - c], d_c)
    back_last(xo)

    down_term(0)
    y_send(0)
    down_term(1)
    y_send(2)
    y_send(1)
    up_exchange()
    down_term(2)
    y_send(3)
    down_term(3)
    up_step(xr)
    up_step(xl)
    up_direct()
    y_forward(0)
    y_forward(2)
    y_send(5)
    up_pass()
    y_send(4)
    combine(0)
    column_onehot()
    z_rest(0)
    combine(2)
    z_rest(2)
    y_forward(3)
    c_w.wait()
    input_grad(0)
    y_forward(5)
    y_forward(1)
    up_split()
    y_forward(4)
    input_grad(1)
    up_cross()
    combine(3)
    combine(4)
    z_rest(4)
    input_grad(2)
    z_rest(3)
    up_own()
    y_send(6)
    combine(1)
    pass_on(3)
    combine(5)
    z_rest(5)
    y_forward(6)
    z_rest(1)
    pass_on(4)
    combine(6)
    pass_on(1)
    pass_on(2)
    pass_on(0)
    input_grad(3)
    pass_on(5)
    finish(3)
    z_rest(6)
    finish(1)
    pass_on(6)
    finish(2)
    finish(5)
    finish(0)
    finish(4)
    finish(6)
    gone(*list(sent))


def drain(ig, dg, ug, ig_h, dg_h, ug_h, sem):
    copies = [pltpu.make_async_copy(src, dst, sem.at[i]) for i, (src, dst) in enumerate(((ig, ig_h), (dg, dg_h), (ug, ug_h)))]
    for copy in copies:
        copy.start()
    for copy in copies:
        copy.wait()


def per_device(tokens, cotangent, value_weight, adapter_down, adapter_up, pair_ids, ranks):
    rows, width = tokens.shape
    norm = 1.0 / math.sqrt(rows * lax.axis_size("pair"))
    cot = cotangent.T
    up = jnp.swapaxes(adapter_up, 1, 2)
    any_spec = pl.BlockSpec(memory_space=pltpu.HBM)
    count = len(NAMES)
    vm = pltpu.VMEM
    import functools
    out = pl.pallas_call(
        functools.partial(kernel, norm),
        out_shape=(
            vm((2048, 512), BF),
            vm((3, 512, 128), BF),
            vm((3, 64, 128), BF),
        ),
        in_specs=[any_spec] * 7,
        out_specs=(pl.BlockSpec(memory_space=pltpu.VMEM),) * 3,
        scratch_shapes=[
            vm((4, 2, 2, 64, 2560), BF),
            vm((2048, 512), BF),
            vm((512, 1024), BF),
            vm((48, 512, 128), BF),
            vm((48, 64, 128), BF),
            vm((4, 512, 128), BF),
            vm((4, 512, 128), BF),
            vm((4, 128, 512), F32),
            vm((4, 128, 512), BF),
            vm((4, 4, 576, 128), BF),
            vm((4, 3, 576, 128), BF),
            vm((3, 288, 128), BF),
            vm((3, 288, 128), BF),
            vm((3, 576, 128), BF),
            vm((3, 576, 128), BF),
            vm((4, 4, 256, 128), BF),
            vm((4, 128, 128), BF),
            vm((4, 128, 128), BF),
            vm((4, 256, 128), BF),
            vm((4, 256, 128), BF),
            vm((2, 2, 4, 64, 128), BF),
            vm((3, 4, 64, 128), BF),
            vm((4, 8, 256), jnp.int32),
            vm((4, 8, 256), jnp.int32),
            vm((2, 192, 256), BF),
            pltpu.SMEM((4,), jnp.int32),
            pltpu.SMEM((48,), jnp.int32),
            pltpu.SemaphoreType.DMA((count,)),
            pltpu.SemaphoreType.DMA((count,)),
            pltpu.SemaphoreType.DMA((7,)),
        ],
        compiler_params=pltpu.CompilerParams(
            collective_id=0, has_side_effects=True, vmem_limit_bytes=60 * 1024 * 1024
        ),
    )(pair_ids, ranks, tokens, cot, value_weight, adapter_down, up)
    out = [pltpu.with_memory_space_constraint(part, pltpu.VMEM) for part in out]
    out = pl.pallas_call(
        drain,
        out_shape=tuple(jax.ShapeDtypeStruct(part.shape, BF) for part in out),
        in_specs=[pl.BlockSpec(memory_space=pltpu.VMEM)] * 3,
        out_specs=(any_spec,) * 3,
        scratch_shapes=[pltpu.SemaphoreType.DMA((3,))],
        compiler_params=pltpu.CompilerParams(vmem_limit_bytes=1024 * 1024),
    )(*out)
    return out[0], out[1], jnp.swapaxes(out[2], 1, 2)


def solution(mesh):
    placed = (
        P("pair", "fsdp"),
        P("pair", "fsdp"),
        P("fsdp", None),
        P(None, "fsdp", None),
        P(None, None, "fsdp"),
        P("pair"),
        P(),
    )
    return jax.shard_map(
        per_device,
        mesh=mesh,
        in_specs=placed,
        out_specs=(P("pair", "fsdp"), P("pair", "fsdp", None), P("pair", None, "fsdp")),
        check_vma=False,
    )
```

```python
import math

import jax
import jax.numpy as jnp
from jax import lax
from jax.experimental import pallas as pl
from jax.experimental.pallas import tpu as pltpu
from jax.sharding import PartitionSpec as P

MESH = pl.DeviceIdType.MESH
BF = jnp.bfloat16
F32 = jnp.float32

NAMES = ["A1", "B1R", "B1L", "B3O", "A2R", "A2L", "A2RZ", "A2LZ", "B2R", "B2L", "B3L", "B3R", "A3R", "A3L", "A3RZ", "A3LZ", "B3F", "C0", "CL", "CR", "CE", "CF"]
NAMES += ["IR", "IL", "IF", "JR", "JL", "JF"]
NAMES += ["X1R", "X1L", "X2Rb", "X2Lb", "X2Ra", "X2La", "Q1", "Q2"]
CHUNKS = [(0, 32), (32, 160), (192, 64), (256, 64), (320, 96), (416, 96), (512, 64)]
SWAPPED = 1
for _k in range(len(CHUNKS)):
    NAMES += [n + str(_k) for n in ("YR", "YL", "YFR", "YFL", "Z1R", "Z1L", "Z2Rb", "Z2Lb", "Z2Ra", "Z2La")]
INDEX = {n: i for i, n in enumerate(NAMES)}


def dot(a, b, ca=1, cb=0):
    return lax.dot_general(a, b, (((ca,), (cb,)), ((), ())), preferred_element_type=F32)


def kernel(norm, ids_h, ranks_h, tok_h, cot_h, w_h, a_h, b_h, igv, dgv, ugv,
           G, xv, wv, av, bv, asel, low, backf, backb, YB, ZB, R1, R2, FL, FR,
           V, XR1, XR2, XFL, XFR, XS, QR, idt, jdt, Lm, ids, ranks, ss, rs, ls):
    f = lax.axis_index("fsdp")
    q = lax.axis_index("pair")
    x, z, c = f // 4, (f // 2) % 2, f % 2
    zh, y = q // 4, q % 4
    xr, xl, xo = (x + 1) % 4, (x + 3) % 4, (x + 2) % 4
    yr, yl, yo = (y + 1) % 4, (y + 3) % 4, (y + 2) % 4
    zr, zl, zo = (zh + 1) % 4, (zh + 3) % 4, (zh + 2) % 4

    def dev(xx, zz, cc):
        return {"fsdp": xx * 4 + zz * 2 + cc}

    def pdev(zz, yy):
        return {"pair": zz * 4 + yy}

    d_z, d_c = dev(x, 1 - z, c), dev(x, z, 1 - c)
    d_xr, d_xl = dev(xr, z, c), dev(xl, z, c)
    d_yr, d_yl = pdev(zh, yr), pdev(zh, yl)
    d_zr, d_zl = pdev(zr, y), pdev(zl, y)

    plain = ((y, yl, yr, yo), d_yl, d_yr, d_zl, d_zr)
    swapped = ((zh, zl, zr, zo), d_zl, d_zr, d_yl, d_yr)
    role = [swapped if k == SWAPPED else plain for k in range(len(CHUNKS))]

    sent = {}

    def send(name, src, dst, device):
        i = INDEX[name]
        copy = pltpu.make_async_remote_copy(src_ref=src, dst_ref=dst, send_sem=ss.at[i], recv_sem=rs.at[i],
                                            device_id=device, device_id_type=MESH)
        copy.start()
        sent[name] = copy

    def gone(*names):
        for name in names:
            sent.pop(name).wait_send()

    def recv(name, dst, device):
        i = INDEX[name]
        pltpu.make_async_remote_copy(src_ref=dst, dst_ref=dst, send_sem=ss.at[i], recv_sem=rs.at[i],
                                     device_id=device, device_id_type=MESH).wait_recv()

    c_cot = pltpu.make_async_copy(cot_h, G.at[x, z, c, :, 0:2048], ls.at[0])
    c_ids = pltpu.make_async_copy(ids_h, ids, ls.at[5])
    c_b = pltpu.make_async_copy(b_h, bv, ls.at[1])
    c_ranks = pltpu.make_async_copy(ranks_h, ranks, ls.at[6])
    for copy in (c_cot, c_ids, c_b, c_ranks):
        copy.start()

    barrier = pltpu.get_barrier_semaphore()
    for device in (d_z, d_c, d_xr, d_xl, d_yr, d_yl, d_zr, d_zl):
        pl.semaphore_signal(barrier, inc=1, device_id=device, device_id_type=MESH)

    c_x = pltpu.make_async_copy(tok_h, xv, ls.at[2])
    c_a = pltpu.make_async_copy(a_h, av, ls.at[3])
    c_w = pltpu.make_async_copy(w_h, wv, ls.at[4])

    L0, L1 = slice(0, 1280), slice(1280, 2560)

    def relay(name, part, device):
        send(name, part, part, device)

    c_cot.wait()
    pl.semaphore_wait(barrier, 8)
    relay("A1", G.at[x, z, c, :, L0], d_z)
    c_b.wait()
    c_ids.wait()
    c_ranks.wait()
    for b in range(4):
        G[x, z, c, :, 2048 + 128 * b:2176 + 128 * b] = bv[ids[b]]
    relay("B1R", G.at[x, z, c, :, L1], d_xr)
    relay("B1L", G.at[x, z, c, :, L1], d_xl)
    relay("B3O", G.at[x, z, c, :, L1], d_z)
    relay("A2R", G.at[x, z, c, :, L0], d_xr)
    relay("A2L", G.at[x, z, c, :, L0], d_xl)
    for copy in (c_x, c_a, c_w):
        copy.start()
    lane = lax.broadcasted_iota(jnp.int32, (8, 256), 1)
    part = (lane >> 4) & 3
    tile = jnp.where(part == 0, ids[0], jnp.where(part == 1, ids[1], jnp.where(part == 2, ids[2], ids[3])))
    idt[y] = tile
    jdt[zh] = tile
    relay("IR", idt.at[y], d_yr)
    relay("IL", idt.at[y], d_yl)
    relay("JR", jdt.at[zh], d_zr)
    relay("JL", jdt.at[zh], d_zl)

    def rank_of(b):
        return ranks[ids[b]]

    def scale_of(b):
        return 32.0 / jnp.broadcast_to(rank_of(b), (1, 128)).astype(F32)

    def features(g, start, count):
        start = pl.multiple_of(start, 128)
        return G[g, :, :, :, pl.ds(start, count)].reshape(256, count)

    def low_all():
        for b in range(4):
            asel[b] = av[ids[b]]

        def body(b, carry):
            value = dot(xv[pl.ds(pl.multiple_of(b * 512, 512), 512), :], asel[b])
            keep = lax.broadcasted_iota(jnp.int32, (512, 128), 1) < rank_of(b)
            low[b] = jnp.where(keep, value, 0.0).astype(BF)
            return carry

        lax.fori_loop(0, 4, body, 0)

    def back_step(g, first):
        for b in range(4):
            value = dot(features(g, 2048 + 128 * b, 128), features(g, 512 * b, 512), 0, 0)
            if first:
                backf[b] = value
            else:
                backf[b] = backf[b] + value

    def back_last(g):
        for b in range(4):
            value = backf[b] + dot(features(g, 2048 + 128 * b, 128), features(g, 512 * b, 512), 0, 0)
            keep = lax.broadcasted_iota(jnp.int32, (128, 512), 0) < rank_of(b)
            backb[b] = jnp.where(keep, value, 0.0).astype(BF)

    def up_step(g):
        def body(b, carry):
            V[g, b] = dot(features(g, 512 * b, 512), low[b]).astype(BF)
            return carry
        lax.fori_loop(0, 4, body, 0)

    def onehot(which):
        row = lax.broadcasted_iota(jnp.int32, (192, 256), 0)
        col = lax.broadcasted_iota(jnp.int32, (192, 256), 1)
        slot = row >> 4
        turn = (slot >= 3).astype(jnp.int32) + (slot >= 6).astype(jnp.int32) + (slot >= 9).astype(jnp.int32)
        if which:
            owner = zh * 4 + ((y + turn) & 3)
        else:
            owner = ((zh + turn) & 3) * 4 + y
        pair = 3 * owner + slot - 3 * turn
        of_block = jnp.zeros((192, 256), jnp.int32)
        table = jdt if which else idt
        for s in range(4):
            of_block = jnp.where((col >> 6) == s, jnp.broadcast_to(table[s][0:1, :], (192, 256)), of_block)
        hit = jnp.logical_and((row & 15) == (col & 15), of_block == pair)
        Lm[which] = jnp.where(hit, 1.0, 0.0).astype(BF)

    def y_send(k):
        r0, n = CHUNKS[k]
        (me, _, _, _), al, ar, _, _ = role[k]
        own = YB.at[me, :, r0:r0 + n]
        relay("YR" + str(k), own, ar)
        relay("YL" + str(k), own, al)

    def y_forward(k):
        r0, n = CHUNKS[k]
        h = n // 2
        (_, il, ir, _), al, ar, _, _ = role[k]
        recv("YR" + str(k), YB.at[il, :, r0:r0 + n], al)
        relay("YFR" + str(k), YB.at[il, :, r0:r0 + h], ar)
        recv("YL" + str(k), YB.at[ir, :, r0:r0 + n], ar)
        relay("YFL" + str(k), YB.at[ir, :, r0 + h:r0 + n], al)

    def combine_math(k):
        r0, n = CHUNKS[k]
        which = 1 if k == SWAPPED else 0

        def body(i, carry):
            top = pl.ds(pl.multiple_of(r0 + 32 * i, 16), 16)
            bottom = pl.ds(pl.multiple_of(r0 + 32 * i + 16, 16), 16)
            stack = jnp.concatenate([YB[:, :, top, :].reshape(256, 128), YB[:, :, bottom, :].reshape(256, 128)], axis=1)
            out = dot(Lm[which], stack).astype(BF)
            ZB[:, :, top, :] = out[:, 0:128].reshape(4, 3, 16, 128)
            ZB[:, :, bottom, :] = out[:, 128:256].reshape(4, 3, 16, 128)
            return carry

        lax.fori_loop(0, n // 32, body, 0)

    def combine(k):
        r0, n = CHUNKS[k]
        h = n // 2
        s0 = r0 // 2
        (_, _, _, io), al, ar, bl, br = role[k]
        recv("YFR" + str(k), YB.at[io, :, r0:r0 + h], al)
        recv("YFL" + str(k), YB.at[io, :, r0 + h:r0 + n], ar)
        combine_math(k)
        send("Z1R" + str(k), ZB.at[2, :, r0:r0 + h], R1.at[:, s0:s0 + h], br)
        send("Z1L" + str(k), ZB.at[2, :, r0 + h:r0 + n], R2.at[:, s0:s0 + h], bl)

    def z_rest(k):
        r0, n = CHUNKS[k]
        h = n // 2
        _, _, _, bl, br = role[k]
        send("Z2Rb" + str(k), ZB.at[1, :, r0 + h:r0 + n], FL.at[:, r0 + h:r0 + n], br)
        send("Z2Lb" + str(k), ZB.at[3, :, r0:r0 + h], FR.at[:, r0:r0 + h], bl)

    def pass_on(k):
        r0, n = CHUNKS[k]
        h = n // 2
        s0 = r0 // 2
        _, _, _, bl, br = role[k]
        recv("Z1R" + str(k), R1.at[:, s0:s0 + h], bl)
        ZB[1, :, r0:r0 + h] = (ZB[1, :, r0:r0 + h].astype(F32) + R1[:, s0:s0 + h].astype(F32)).astype(BF)
        send("Z2Ra" + str(k), ZB.at[1, :, r0:r0 + h], FL.at[:, r0:r0 + h], br)
        recv("Z1L" + str(k), R2.at[:, s0:s0 + h], br)
        ZB[3, :, r0 + h:r0 + n] = (ZB[3, :, r0 + h:r0 + n].astype(F32) + R2[:, s0:s0 + h].astype(F32)).astype(BF)
        send("Z2La" + str(k), ZB.at[3, :, r0 + h:r0 + n], FR.at[:, r0 + h:r0 + n], bl)

    def finish(k):
        r0, n = CHUNKS[k]
        h = n // 2
        _, _, _, bl, br = role[k]
        recv("Z2Rb" + str(k), FL.at[:, r0 + h:r0 + n], bl)
        recv("Z2Lb" + str(k), FR.at[:, r0:r0 + h], br)
        recv("Z2Ra" + str(k), FL.at[:, r0:r0 + h], bl)
        recv("Z2La" + str(k), FR.at[:, r0 + h:r0 + n], br)
        total = (ZB[0, :, r0:r0 + n].astype(F32) + FL[:, r0:r0 + n].astype(F32) + FR[:, r0:r0 + n].astype(F32)).astype(BF)
        if r0 < 512:
            dgv[:, r0:r0 + n] = total
        else:
            ugv[...] = total

    def down_term(k):
        for b in range(4):
            value = dot(backb[b], xv[512 * b:512 * b + 512, 128 * k:128 * k + 128])
            value = (value.T * (scale_of(b) * norm)).astype(BF)
            for i, (r0, n) in enumerate(CHUNKS):
                lo, hi = max(r0, 128 * k), min(r0 + n, 128 * k + 128)
                if lo < hi:
                    YB[role[i][0][0], b, lo:hi, :] = value[lo - 128 * k:hi - 128 * k]

    def input_grad(b):
        ad = scale_of(b)[:, 0:1]

        def body(i, carry):
            rows = pl.ds(pl.multiple_of(i * 128, 128), 128)
            acc = dot(wv[rows, 0:256], features(0, 512 * b, 512))
            for g in range(1, 4):
                acc = acc + dot(wv[rows, 256 * g:256 * g + 256], features(g, 512 * b, 512))
            extra = dot(asel[b, rows, :], backb[b])
            value = acc.astype(BF).astype(F32) + ad * extra
            igv[512 * b:512 * b + 512, rows] = value.T.astype(BF)
            return carry

        lax.fori_loop(0, 4, body, 0)

    me, other = c, 1 - c

    def up_exchange():
        up_step(xo)
        send("X1R", V.at[xo, :, 0:128], XR1, d_xr)
        send("X1L", V.at[xo, :, 128:256], XR2, d_xl)

    def up_direct():
        send("X2Rb", V.at[xr, :, 128:256], XFL.at[:, 128:256], d_xr)
        send("X2Lb", V.at[xl, :, 0:128], XFR.at[:, 0:128], d_xl)

    def up_pass():
        recv("X1R", XR1, d_xl)
        V[xr, :, 0:128] = (V[xr, :, 0:128].astype(F32) + XR1[...].astype(F32)).astype(BF)
        send("X2Ra", V.at[xr, :, 0:128], XFL.at[:, 0:128], d_xr)
        recv("X1L", XR2, d_xr)
        V[xl, :, 128:256] = (V[xl, :, 128:256].astype(F32) + XR2[...].astype(F32)).astype(BF)
        send("X2La", V.at[xl, :, 128:256], XFR.at[:, 128:256], d_xl)

    def up_split():
        recv("X2Rb", XFL.at[:, 128:256], d_xl)
        recv("X2Lb", XFR.at[:, 0:128], d_xr)
        recv("X2Ra", XFL.at[:, 0:128], d_xl)
        recv("X2La", XFR.at[:, 128:256], d_xr)
        for s in range(4):
            rows = slice(64 * s, 64 * s + 64)
            total = V[x, :, rows].astype(F32) + XFL[:, rows].astype(F32) + XFR[:, rows].astype(F32)
            XS[s % 2, s // 2] = total.astype(BF)
        send("Q2", XS.at[other], QR.at[0:2], d_c)

    def up_cross():
        recv("Q2", QR.at[0:2], d_c)
        XS[me, 1 - z] = (XS[me, 1 - z].astype(F32) + QR[1 - z].astype(F32)).astype(BF)
        send("Q1", XS.at[me, 1 - z], QR.at[2], d_z)

    def up_own():
        recv("Q1", QR.at[2], d_z)

        def body(b, carry):
            total = XS[me, z, b].astype(F32) + QR[z, b].astype(F32) + QR[2, b].astype(F32)
            YB[y, b, 512:576, :] = (total * (scale_of(b) * norm)).astype(BF)
            return carry

        lax.fori_loop(0, 4, body, 0)

    def column_onehot():
        recv("JL", jdt.at[zr], d_zr)
        recv("JF", jdt.at[zo], d_zl)
        onehot(1)

    c_a.wait()
    c_x.wait()
    low_all()
    recv("B1R", G.at[xl, z, c, :, L1], d_xl)
    relay("B2R", G.at[xl, z, c, 0:32, L1], d_xr)
    relay("B3L", G.at[xl, z, c, :, L1], d_z)
    recv("B1L", G.at[xr, z, c, :, L1], d_xr)
    relay("B2L", G.at[xr, z, c, 32:64, L1], d_xl)
    relay("B3R", G.at[xr, z, c, :, L1], d_z)
    recv("A1", G.at[x, 1 - z, c, :, L0], d_z)
    relay("A2RZ", G.at[x, 1 - z, c, :, L0], d_xr)
    relay("A2LZ", G.at[x, 1 - z, c, :, L0], d_xl)
    recv("IR", idt.at[yl], d_yl)
    relay("IF", idt.at[yl], d_yr)
    recv("B3O", G.at[x, 1 - z, c, :, L1], d_z)
    relay("C0", G.at[x, :, c], d_c)
    recv("A2R", G.at[xl, z, c, :, L0], d_xl)
    relay("A3R", G.at[xl, z, c, 0:32, L0], d_xr)
    recv("A2L", G.at[xr, z, c, :, L0], d_xr)
    relay("A3L", G.at[xr, z, c, 32:64, L0], d_xl)
    recv("B2R", G.at[xo, z, c, 0:32, L1], d_xl)
    recv("B2L", G.at[xo, z, c, 32:64, L1], d_xr)
    relay("B3F", G.at[xo, z, c, :, L1], d_z)
    recv("C0", G.at[x, :, 1 - c], d_c)
    back_step(x, True)
    up_step(x)
    recv("IL", idt.at[yr], d_yr)
    recv("IF", idt.at[yo], d_yl)
    onehot(0)
    recv("A2RZ", G.at[xl, 1 - z, c, :, L0], d_xl)
    relay("A3RZ", G.at[xl, 1 - z, c, 0:32, L0], d_xr)
    recv("A2LZ", G.at[xr, 1 - z, c, :, L0], d_xr)
    relay("A3LZ", G.at[xr, 1 - z, c, 32:64, L0], d_xl)
    recv("B3L", G.at[xl, 1 - z, c, :, L1], d_z)
    relay("CL", G.at[xl, :, c], d_c)
    recv("B3R", G.at[xr, 1 - z, c, :, L1], d_z)
    relay("CR", G.at[xr, :, c], d_c)
    recv("A3R", G.at[xo, z, c, 0:32, L0], d_xl)
    recv("A3L", G.at[xo, z, c, 32:64, L0], d_xr)
    relay("CE", G.at[xo, z, c], d_c)
    recv("JR", jdt.at[zl], d_zl)
    relay("JF", jdt.at[zl], d_zr)
    recv("CL", G.at[xl, :, 1 - c], d_c)
    back_step(xl, False)
    recv("A3RZ", G.at[xo, 1 - z, c, 0:32, L0], d_xl)
    recv("A3LZ", G.at[xo, 1 - z, c, 32:64, L0], d_xr)
    recv("B3F", G.at[xo, 1 - z, c, :, L1], d_z)
    relay("CF", G.at[xo, 1 - z, c], d_c)
    recv("CR", G.at[xr, :, 1 - c], d_c)
    back_step(xr, False)
    recv("CE", G.at[xo, z, 1 - c], d_c)
    recv("CF", G.at[xo, 1 - z, 1 - c], d_c)
    back_last(xo)

    down_term(0)
    y_send(0)
    down_term(1)
    y_send(2)
    y_send(1)
    up_exchange()
    down_term(2)
    y_send(3)
    down_term(3)
    up_step(xr)
    up_step(xl)
    up_direct()
    y_forward(0)
    y_forward(2)
    y_send(5)
    up_pass()
    y_send(4)
    combine(0)
    column_onehot()
    z_rest(0)
    combine(2)
    z_rest(2)
    y_forward(3)
    c_w.wait()
    input_grad(0)
    y_forward(5)
    y_forward(1)
    up_split()
    y_forward(4)
    input_grad(1)
    up_cross()
    combine(3)
    combine(4)
    z_rest(4)
    input_grad(2)
    z_rest(3)
    up_own()
    y_send(6)
    combine(1)
    pass_on(3)
    combine(5)
    z_rest(5)
    y_forward(6)
    z_rest(1)
    pass_on(4)
    combine(6)
    pass_on(1)
    pass_on(2)
    pass_on(0)
    input_grad(3)
    pass_on(5)
    finish(3)
    z_rest(6)
    finish(1)
    pass_on(6)
    finish(2)
    finish(5)
    finish(0)
    finish(4)
    finish(6)
    gone(*list(sent))


def drain(ig, dg, ug, ig_h, dg_h, ug_h, sem):
    copies = [pltpu.make_async_copy(src, dst, sem.at[i]) for i, (src, dst) in enumerate(((ig, ig_h), (dg, dg_h), (ug, ug_h)))]
    for copy in copies:
        copy.start()
    for copy in copies:
        copy.wait()


def per_device(tokens, cotangent, value_weight, adapter_down, adapter_up, pair_ids, ranks):
    rows, width = tokens.shape
    norm = 1.0 / math.sqrt(rows * lax.axis_size("pair"))
    cot = cotangent.T
    up = jnp.swapaxes(adapter_up, 1, 2)
    any_spec = pl.BlockSpec(memory_space=pltpu.HBM)
    count = len(NAMES)
    vm = pltpu.VMEM
    import functools
    out = pl.pallas_call(
        functools.partial(kernel, norm),
        out_shape=(
            vm((2048, 512), BF),
            vm((3, 512, 128), BF),
            vm((3, 64, 128), BF),
        ),
        in_specs=[any_spec] * 7,
        out_specs=(pl.BlockSpec(memory_space=pltpu.VMEM),) * 3,
        scratch_shapes=[
            vm((4, 2, 2, 64, 2560), BF),
            vm((2048, 512), BF),
            vm((512, 1024), BF),
            vm((48, 512, 128), BF),
            vm((48, 64, 128), BF),
            vm((4, 512, 128), BF),
            vm((4, 512, 128), BF),
            vm((4, 128, 512), F32),
            vm((4, 128, 512), BF),
            vm((4, 4, 576, 128), BF),
            vm((4, 3, 576, 128), BF),
            vm((3, 288, 128), BF),
            vm((3, 288, 128), BF),
            vm((3, 576, 128), BF),
            vm((3, 576, 128), BF),
            vm((4, 4, 256, 128), BF),
            vm((4, 128, 128), BF),
            vm((4, 128, 128), BF),
            vm((4, 256, 128), BF),
            vm((4, 256, 128), BF),
            vm((2, 2, 4, 64, 128), BF),
            vm((3, 4, 64, 128), BF),
            vm((4, 8, 256), jnp.int32),
            vm((4, 8, 256), jnp.int32),
            vm((2, 192, 256), BF),
            pltpu.SMEM((4,), jnp.int32),
            pltpu.SMEM((48,), jnp.int32),
            pltpu.SemaphoreType.DMA((count,)),
            pltpu.SemaphoreType.DMA((count,)),
            pltpu.SemaphoreType.DMA((7,)),
        ],
        compiler_params=pltpu.CompilerParams(
            collective_id=0, has_side_effects=True, vmem_limit_bytes=60 * 1024 * 1024
        ),
    )(pair_ids, ranks, tokens, cot, value_weight, adapter_down, up)
    out = [pltpu.with_memory_space_constraint(part, pltpu.VMEM) for part in out]
    out = pl.pallas_call(
        drain,
        out_shape=tuple(jax.ShapeDtypeStruct(part.shape, BF) for part in out),
        in_specs=[pl.BlockSpec(memory_space=pltpu.VMEM)] * 3,
        out_specs=(any_spec,) * 3,
        scratch_shapes=[pltpu.SemaphoreType.DMA((3,))],
        compiler_params=pltpu.CompilerParams(vmem_limit_bytes=1024 * 1024),
    )(*out)
    return out[0], out[1], jnp.swapaxes(out[2], 1, 2)


def solution(mesh):
    placed = (
        P("pair", "fsdp"),
        P("pair", "fsdp"),
        P("fsdp", None),
        P(None, "fsdp", None),
        P(None, None, "fsdp"),
        P("pair"),
        P(),
    )
    return jax.shard_map(
        per_device,
        mesh=mesh,
        in_specs=placed,
        out_specs=(P("pair", "fsdp"), P("pair", "fsdp", None), P("pair", None, "fsdp")),
        check_vma=False,
    )
```

```python
import math

import jax
import jax.numpy as jnp
from jax import lax
from jax.experimental import pallas as pl
from jax.experimental.pallas import tpu as pltpu
from jax.sharding import PartitionSpec as P

MESH = pl.DeviceIdType.MESH
BF = jnp.bfloat16
F32 = jnp.float32

NAMES = ["A1", "B1R", "B1L", "B3O", "A2R", "A2L", "A2RZ", "A2LZ", "B2R", "B2L", "B3L", "B3R", "A3R", "A3L", "A3RZ", "A3LZ", "B3F", "C0", "CL", "CR", "CE", "CF"]
NAMES += ["IR", "IL", "IF", "JR", "JL", "JF"]
NAMES += ["X1R", "X1L", "X2Rb", "X2Lb", "X2Ra", "X2La", "Q1", "Q2"]
CHUNKS = [(0, 32), (32, 160), (192, 64), (256, 96), (352, 96), (448, 64), (512, 64)]
SWAPPED = 1
for _k in range(len(CHUNKS)):
    NAMES += [n + str(_k) for n in ("YR", "YL", "YFR", "YFL", "Z1R", "Z1L", "Z2Rb", "Z2Lb", "Z2Ra", "Z2La")]
INDEX = {n: i for i, n in enumerate(NAMES)}


def dot(a, b, ca=1, cb=0):
    return lax.dot_general(a, b, (((ca,), (cb,)), ((), ())), preferred_element_type=F32)


def kernel(norm, ids_h, ranks_h, tok_h, cot_h, w_h, a_h, b_h, igv, dgv, ugv,
           G, xv, wv, av, bv, asel, low, backf, backb, YB, ZB, R1, R2, FL, FR,
           V, XR1, XR2, XFL, XFR, XS, QR, idt, jdt, Lm, ids, ranks, ss, rs, ls):
    f = lax.axis_index("fsdp")
    q = lax.axis_index("pair")
    x, z, c = f // 4, (f // 2) % 2, f % 2
    zh, y = q // 4, q % 4
    xr, xl, xo = (x + 1) % 4, (x + 3) % 4, (x + 2) % 4
    yr, yl, yo = (y + 1) % 4, (y + 3) % 4, (y + 2) % 4
    zr, zl, zo = (zh + 1) % 4, (zh + 3) % 4, (zh + 2) % 4

    def dev(xx, zz, cc):
        return {"fsdp": xx * 4 + zz * 2 + cc}

    def pdev(zz, yy):
        return {"pair": zz * 4 + yy}

    d_z, d_c = dev(x, 1 - z, c), dev(x, z, 1 - c)
    d_xr, d_xl = dev(xr, z, c), dev(xl, z, c)
    d_yr, d_yl = pdev(zh, yr), pdev(zh, yl)
    d_zr, d_zl = pdev(zr, y), pdev(zl, y)

    plain = ((y, yl, yr, yo), d_yl, d_yr, d_zl, d_zr)
    swapped = ((zh, zl, zr, zo), d_zl, d_zr, d_yl, d_yr)
    role = [swapped if k == SWAPPED else plain for k in range(len(CHUNKS))]

    sent = {}

    def send(name, src, dst, device):
        i = INDEX[name]
        copy = pltpu.make_async_remote_copy(src_ref=src, dst_ref=dst, send_sem=ss.at[i], recv_sem=rs.at[i],
                                            device_id=device, device_id_type=MESH)
        copy.start()
        sent[name] = copy

    def gone(*names):
        for name in names:
            sent.pop(name).wait_send()

    def recv(name, dst, device):
        i = INDEX[name]
        pltpu.make_async_remote_copy(src_ref=dst, dst_ref=dst, send_sem=ss.at[i], recv_sem=rs.at[i],
                                     device_id=device, device_id_type=MESH).wait_recv()

    c_cot = pltpu.make_async_copy(cot_h, G.at[x, z, c, :, 0:2048], ls.at[0])
    c_ids = pltpu.make_async_copy(ids_h, ids, ls.at[5])
    c_b = pltpu.make_async_copy(b_h, bv, ls.at[1])
    c_ranks = pltpu.make_async_copy(ranks_h, ranks, ls.at[6])
    for copy in (c_cot, c_ids, c_b, c_ranks):
        copy.start()

    barrier = pltpu.get_barrier_semaphore()
    for device in (d_z, d_c, d_xr, d_xl, d_yr, d_yl, d_zr, d_zl):
        pl.semaphore_signal(barrier, inc=1, device_id=device, device_id_type=MESH)

    c_x = pltpu.make_async_copy(tok_h, xv, ls.at[2])
    c_a = pltpu.make_async_copy(a_h, av, ls.at[3])
    c_w = pltpu.make_async_copy(w_h, wv, ls.at[4])

    L0, L1 = slice(0, 1280), slice(1280, 2560)

    def relay(name, part, device):
        send(name, part, part, device)

    c_cot.wait()
    pl.semaphore_wait(barrier, 8)
    relay("A1", G.at[x, z, c, :, L0], d_z)
    c_b.wait()
    c_ids.wait()
    c_ranks.wait()
    for b in range(4):
        G[x, z, c, :, 2048 + 128 * b:2176 + 128 * b] = bv[ids[b]]
    relay("B1R", G.at[x, z, c, :, L1], d_xr)
    relay("B1L", G.at[x, z, c, :, L1], d_xl)
    relay("B3O", G.at[x, z, c, :, L1], d_z)
    relay("A2R", G.at[x, z, c, :, L0], d_xr)
    relay("A2L", G.at[x, z, c, :, L0], d_xl)
    for copy in (c_x, c_a, c_w):
        copy.start()
    lane = lax.broadcasted_iota(jnp.int32, (8, 256), 1)
    part = (lane >> 4) & 3
    tile = jnp.where(part == 0, ids[0], jnp.where(part == 1, ids[1], jnp.where(part == 2, ids[2], ids[3])))
    idt[y] = tile
    jdt[zh] = tile
    relay("IR", idt.at[y], d_yr)
    relay("IL", idt.at[y], d_yl)
    relay("JR", jdt.at[zh], d_zr)
    relay("JL", jdt.at[zh], d_zl)

    def rank_of(b):
        return ranks[ids[b]]

    def scale_of(b):
        return 32.0 / jnp.broadcast_to(rank_of(b), (1, 128)).astype(F32)

    def features(g, start, count):
        start = pl.multiple_of(start, 128)
        return G[g, :, :, :, pl.ds(start, count)].reshape(256, count)

    def low_all():
        for b in range(4):
            asel[b] = av[ids[b]]

        def body(b, carry):
            value = dot(xv[pl.ds(pl.multiple_of(b * 512, 512), 512), :], asel[b])
            keep = lax.broadcasted_iota(jnp.int32, (512, 128), 1) < rank_of(b)
            low[b] = jnp.where(keep, value, 0.0).astype(BF)
            return carry

        lax.fori_loop(0, 4, body, 0)

    def back_step(g, first):
        for b in range(4):
            value = dot(features(g, 2048 + 128 * b, 128), features(g, 512 * b, 512), 0, 0)
            if first:
                backf[b] = value
            else:
                backf[b] = backf[b] + value

    def back_last(g):
        for b in range(4):
            value = backf[b] + dot(features(g, 2048 + 128 * b, 128), features(g, 512 * b, 512), 0, 0)
            keep = lax.broadcasted_iota(jnp.int32, (128, 512), 0) < rank_of(b)
            backb[b] = jnp.where(keep, value, 0.0).astype(BF)

    def up_step(g):
        def body(b, carry):
            V[g, b] = dot(features(g, 512 * b, 512), low[b]).astype(BF)
            return carry
        lax.fori_loop(0, 4, body, 0)

    def onehot(which):
        row = lax.broadcasted_iota(jnp.int32, (192, 256), 0)
        col = lax.broadcasted_iota(jnp.int32, (192, 256), 1)
        slot = row >> 4
        turn = (slot >= 3).astype(jnp.int32) + (slot >= 6).astype(jnp.int32) + (slot >= 9).astype(jnp.int32)
        if which:
            owner = zh * 4 + ((y + turn) & 3)
        else:
            owner = ((zh + turn) & 3) * 4 + y
        pair = 3 * owner + slot - 3 * turn
        of_block = jnp.zeros((192, 256), jnp.int32)
        table = jdt if which else idt
        for s in range(4):
            of_block = jnp.where((col >> 6) == s, jnp.broadcast_to(table[s][0:1, :], (192, 256)), of_block)
        hit = jnp.logical_and((row & 15) == (col & 15), of_block == pair)
        Lm[which] = jnp.where(hit, 1.0, 0.0).astype(BF)

    def y_send(k):
        r0, n = CHUNKS[k]
        (me, _, _, _), al, ar, _, _ = role[k]
        own = YB.at[me, :, r0:r0 + n]
        relay("YR" + str(k), own, ar)
        relay("YL" + str(k), own, al)

    def y_forward(k):
        r0, n = CHUNKS[k]
        h = n // 2
        (_, il, ir, _), al, ar, _, _ = role[k]
        recv("YR" + str(k), YB.at[il, :, r0:r0 + n], al)
        relay("YFR" + str(k), YB.at[il, :, r0:r0 + h], ar)
        recv("YL" + str(k), YB.at[ir, :, r0:r0 + n], ar)
        relay("YFL" + str(k), YB.at[ir, :, r0 + h:r0 + n], al)

    def combine_math(k):
        r0, n = CHUNKS[k]
        which = 1 if k == SWAPPED else 0

        def body(i, carry):
            top = pl.ds(pl.multiple_of(r0 + 32 * i, 16), 16)
            bottom = pl.ds(pl.multiple_of(r0 + 32 * i + 16, 16), 16)
            stack = jnp.concatenate([YB[:, :, top, :].reshape(256, 128), YB[:, :, bottom, :].reshape(256, 128)], axis=1)
            out = dot(Lm[which], stack).astype(BF)
            ZB[:, :, top, :] = out[:, 0:128].reshape(4, 3, 16, 128)
            ZB[:, :, bottom, :] = out[:, 128:256].reshape(4, 3, 16, 128)
            return carry

        lax.fori_loop(0, n // 32, body, 0)

    def combine(k):
        r0, n = CHUNKS[k]
        h = n // 2
        s0 = r0 // 2
        (_, _, _, io), al, ar, bl, br = role[k]
        recv("YFR" + str(k), YB.at[io, :, r0:r0 + h], al)
        recv("YFL" + str(k), YB.at[io, :, r0 + h:r0 + n], ar)
        combine_math(k)
        send("Z1R" + str(k), ZB.at[2, :, r0:r0 + h], R1.at[:, s0:s0 + h], br)
        send("Z1L" + str(k), ZB.at[2, :, r0 + h:r0 + n], R2.at[:, s0:s0 + h], bl)

    def z_rest(k):
        r0, n = CHUNKS[k]
        h = n // 2
        _, _, _, bl, br = role[k]
        send("Z2Rb" + str(k), ZB.at[1, :, r0 + h:r0 + n], FL.at[:, r0 + h:r0 + n], br)
        send("Z2Lb" + str(k), ZB.at[3, :, r0:r0 + h], FR.at[:, r0:r0 + h], bl)

    def pass_on(k):
        r0, n = CHUNKS[k]
        h = n // 2
        s0 = r0 // 2
        _, _, _, bl, br = role[k]
        recv("Z1R" + str(k), R1.at[:, s0:s0 + h], bl)
        ZB[1, :, r0:r0 + h] = (ZB[1, :, r0:r0 + h].astype(F32) + R1[:, s0:s0 + h].astype(F32)).astype(BF)
        send("Z2Ra" + str(k), ZB.at[1, :, r0:r0 + h], FL.at[:, r0:r0 + h], br)
        recv("Z1L" + str(k), R2.at[:, s0:s0 + h], br)
        ZB[3, :, r0 + h:r0 + n] = (ZB[3, :, r0 + h:r0 + n].astype(F32) + R2[:, s0:s0 + h].astype(F32)).astype(BF)
        send("Z2La" + str(k), ZB.at[3, :, r0 + h:r0 + n], FR.at[:, r0 + h:r0 + n], bl)

    def finish(k):
        r0, n = CHUNKS[k]
        h = n // 2
        _, _, _, bl, br = role[k]
        recv("Z2Rb" + str(k), FL.at[:, r0 + h:r0 + n], bl)
        recv("Z2Lb" + str(k), FR.at[:, r0:r0 + h], br)
        recv("Z2Ra" + str(k), FL.at[:, r0:r0 + h], bl)
        recv("Z2La" + str(k), FR.at[:, r0 + h:r0 + n], br)
        total = (ZB[0, :, r0:r0 + n].astype(F32) + FL[:, r0:r0 + n].astype(F32) + FR[:, r0:r0 + n].astype(F32)).astype(BF)
        if r0 < 512:
            dgv[:, r0:r0 + n] = total
        else:
            ugv[...] = total

    def down_term(k):
        for b in range(4):
            value = dot(backb[b], xv[512 * b:512 * b + 512, 128 * k:128 * k + 128])
            value = (value.T * (scale_of(b) * norm)).astype(BF)
            for i, (r0, n) in enumerate(CHUNKS):
                lo, hi = max(r0, 128 * k), min(r0 + n, 128 * k + 128)
                if lo < hi:
                    YB[role[i][0][0], b, lo:hi, :] = value[lo - 128 * k:hi - 128 * k]

    def input_grad(b):
        ad = scale_of(b)[:, 0:1]

        def body(i, carry):
            rows = pl.ds(pl.multiple_of(i * 128, 128), 128)
            acc = dot(wv[rows, 0:256], features(0, 512 * b, 512))
            for g in range(1, 4):
                acc = acc + dot(wv[rows, 256 * g:256 * g + 256], features(g, 512 * b, 512))
            extra = dot(asel[b, rows, :], backb[b])
            value = acc.astype(BF).astype(F32) + ad * extra
            igv[512 * b:512 * b + 512, rows] = value.T.astype(BF)
            return carry

        lax.fori_loop(0, 4, body, 0)

    me, other = c, 1 - c

    def up_exchange():
        up_step(xo)
        send("X1R", V.at[xo, :, 0:128], XR1, d_xr)
        send("X1L", V.at[xo, :, 128:256], XR2, d_xl)

    def up_direct():
        send("X2Rb", V.at[xr, :, 128:256], XFL.at[:, 128:256], d_xr)
        send("X2Lb", V.at[xl, :, 0:128], XFR.at[:, 0:128], d_xl)

    def up_pass():
        recv("X1R", XR1, d_xl)
        V[xr, :, 0:128] = (V[xr, :, 0:128].astype(F32) + XR1[...].astype(F32)).astype(BF)
        send("X2Ra", V.at[xr, :, 0:128], XFL.at[:, 0:128], d_xr)
        recv("X1L", XR2, d_xr)
        V[xl, :, 128:256] = (V[xl, :, 128:256].astype(F32) + XR2[...].astype(F32)).astype(BF)
        send("X2La", V.at[xl, :, 128:256], XFR.at[:, 128:256], d_xl)

    def up_split():
        recv("X2Rb", XFL.at[:, 128:256], d_xl)
        recv("X2Lb", XFR.at[:, 0:128], d_xr)
        recv("X2Ra", XFL.at[:, 0:128], d_xl)
        recv("X2La", XFR.at[:, 128:256], d_xr)
        for s in range(4):
            rows = slice(64 * s, 64 * s + 64)
            total = V[x, :, rows].astype(F32) + XFL[:, rows].astype(F32) + XFR[:, rows].astype(F32)
            XS[s % 2, s // 2] = total.astype(BF)
        send("Q2", XS.at[other], QR.at[0:2], d_c)

    def up_cross():
        recv("Q2", QR.at[0:2], d_c)
        XS[me, 1 - z] = (XS[me, 1 - z].astype(F32) + QR[1 - z].astype(F32)).astype(BF)
        send("Q1", XS.at[me, 1 - z], QR.at[2], d_z)

    def up_own():
        recv("Q1", QR.at[2], d_z)

        def body(b, carry):
            total = XS[me, z, b].astype(F32) + QR[z, b].astype(F32) + QR[2, b].astype(F32)
            YB[y, b, 512:576, :] = (total * (scale_of(b) * norm)).astype(BF)
            return carry

        lax.fori_loop(0, 4, body, 0)

    def column_onehot():
        recv("JL", jdt.at[zr], d_zr)
        recv("JF", jdt.at[zo], d_zl)
        onehot(1)

    c_a.wait()
    c_x.wait()
    low_all()
    recv("B1R", G.at[xl, z, c, :, L1], d_xl)
    relay("B2R", G.at[xl, z, c, 0:32, L1], d_xr)
    relay("B3L", G.at[xl, z, c, :, L1], d_z)
    recv("B1L", G.at[xr, z, c, :, L1], d_xr)
    relay("B2L", G.at[xr, z, c, 32:64, L1], d_xl)
    relay("B3R", G.at[xr, z, c, :, L1], d_z)
    recv("A1", G.at[x, 1 - z, c, :, L0], d_z)
    relay("A2RZ", G.at[x, 1 - z, c, :, L0], d_xr)
    relay("A2LZ", G.at[x, 1 - z, c, :, L0], d_xl)
    recv("IR", idt.at[yl], d_yl)
    relay("IF", idt.at[yl], d_yr)
    recv("B3O", G.at[x, 1 - z, c, :, L1], d_z)
    relay("C0", G.at[x, :, c], d_c)
    recv("A2R", G.at[xl, z, c, :, L0], d_xl)
    relay("A3R", G.at[xl, z, c, 0:32, L0], d_xr)
    recv("A2L", G.at[xr, z, c, :, L0], d_xr)
    relay("A3L", G.at[xr, z, c, 32:64, L0], d_xl)
    recv("B2R", G.at[xo, z, c, 0:32, L1], d_xl)
    recv("B2L", G.at[xo, z, c, 32:64, L1], d_xr)
    relay("B3F", G.at[xo, z, c, :, L1], d_z)
    recv("C0", G.at[x, :, 1 - c], d_c)
    back_step(x, True)
    up_step(x)
    recv("IL", idt.at[yr], d_yr)
    recv("IF", idt.at[yo], d_yl)
    onehot(0)
    recv("A2RZ", G.at[xl, 1 - z, c, :, L0], d_xl)
    relay("A3RZ", G.at[xl, 1 - z, c, 0:32, L0], d_xr)
    recv("A2LZ", G.at[xr, 1 - z, c, :, L0], d_xr)
    relay("A3LZ", G.at[xr, 1 - z, c, 32:64, L0], d_xl)
    recv("B3L", G.at[xl, 1 - z, c, :, L1], d_z)
    relay("CL", G.at[xl, :, c], d_c)
    recv("B3R", G.at[xr, 1 - z, c, :, L1], d_z)
    relay("CR", G.at[xr, :, c], d_c)
    recv("A3R", G.at[xo, z, c, 0:32, L0], d_xl)
    recv("A3L", G.at[xo, z, c, 32:64, L0], d_xr)
    relay("CE", G.at[xo, z, c], d_c)
    recv("JR", jdt.at[zl], d_zl)
    relay("JF", jdt.at[zl], d_zr)
    recv("CL", G.at[xl, :, 1 - c], d_c)
    back_step(xl, False)
    recv("A3RZ", G.at[xo, 1 - z, c, 0:32, L0], d_xl)
    recv("A3LZ", G.at[xo, 1 - z, c, 32:64, L0], d_xr)
    recv("B3F", G.at[xo, 1 - z, c, :, L1], d_z)
    relay("CF", G.at[xo, 1 - z, c], d_c)
    recv("CR", G.at[xr, :, 1 - c], d_c)
    back_step(xr, False)
    recv("CE", G.at[xo, z, 1 - c], d_c)
    recv("CF", G.at[xo, 1 - z, 1 - c], d_c)
    back_last(xo)

    down_term(0)
    y_send(0)
    down_term(1)
    y_send(2)
    y_send(1)
    up_exchange()
    down_term(2)
    y_send(3)
    down_term(3)
    up_step(xr)
    up_step(xl)
    up_direct()
    y_forward(0)
    y_forward(2)
    y_send(5)
    up_pass()
    y_send(4)
    combine(0)
    column_onehot()
    z_rest(0)
    combine(2)
    z_rest(2)
    y_forward(3)
    c_w.wait()
    input_grad(0)
    y_forward(5)
    y_forward(1)
    up_split()
    y_forward(4)
    input_grad(1)
    up_cross()
    combine(3)
    combine(4)
    z_rest(4)
    input_grad(2)
    z_rest(3)
    up_own()
    y_send(6)
    combine(1)
    pass_on(3)
    combine(5)
    z_rest(5)
    y_forward(6)
    z_rest(1)
    pass_on(4)
    combine(6)
    pass_on(1)
    pass_on(2)
    pass_on(0)
    input_grad(3)
    pass_on(5)
    finish(3)
    z_rest(6)
    finish(1)
    pass_on(6)
    finish(2)
    finish(5)
    finish(0)
    finish(4)
    finish(6)
    gone(*list(sent))


def drain(ig, dg, ug, ig_h, dg_h, ug_h, sem):
    copies = [pltpu.make_async_copy(src, dst, sem.at[i]) for i, (src, dst) in enumerate(((ig, ig_h), (dg, dg_h), (ug, ug_h)))]
    for copy in copies:
        copy.start()
    for copy in copies:
        copy.wait()


def per_device(tokens, cotangent, value_weight, adapter_down, adapter_up, pair_ids, ranks):
    rows, width = tokens.shape
    norm = 1.0 / math.sqrt(rows * lax.axis_size("pair"))
    cot = cotangent.T
    up = jnp.swapaxes(adapter_up, 1, 2)
    any_spec = pl.BlockSpec(memory_space=pltpu.HBM)
    count = len(NAMES)
    vm = pltpu.VMEM
    import functools
    out = pl.pallas_call(
        functools.partial(kernel, norm),
        out_shape=(
            vm((2048, 512), BF),
            vm((3, 512, 128), BF),
            vm((3, 64, 128), BF),
        ),
        in_specs=[any_spec] * 7,
        out_specs=(pl.BlockSpec(memory_space=pltpu.VMEM),) * 3,
        scratch_shapes=[
            vm((4, 2, 2, 64, 2560), BF),
            vm((2048, 512), BF),
            vm((512, 1024), BF),
            vm((48, 512, 128), BF),
            vm((48, 64, 128), BF),
            vm((4, 512, 128), BF),
            vm((4, 512, 128), BF),
            vm((4, 128, 512), F32),
            vm((4, 128, 512), BF),
            vm((4, 4, 576, 128), BF),
            vm((4, 3, 576, 128), BF),
            vm((3, 288, 128), BF),
            vm((3, 288, 128), BF),
            vm((3, 576, 128), BF),
            vm((3, 576, 128), BF),
            vm((4, 4, 256, 128), BF),
            vm((4, 128, 128), BF),
            vm((4, 128, 128), BF),
            vm((4, 256, 128), BF),
            vm((4, 256, 128), BF),
            vm((2, 2, 4, 64, 128), BF),
            vm((3, 4, 64, 128), BF),
            vm((4, 8, 256), jnp.int32),
            vm((4, 8, 256), jnp.int32),
            vm((2, 192, 256), BF),
            pltpu.SMEM((4,), jnp.int32),
            pltpu.SMEM((48,), jnp.int32),
            pltpu.SemaphoreType.DMA((count,)),
            pltpu.SemaphoreType.DMA((count,)),
            pltpu.SemaphoreType.DMA((7,)),
        ],
        compiler_params=pltpu.CompilerParams(
            collective_id=0, has_side_effects=True, vmem_limit_bytes=60 * 1024 * 1024
        ),
    )(pair_ids, ranks, tokens, cot, value_weight, adapter_down, up)
    out = [pltpu.with_memory_space_constraint(part, pltpu.VMEM) for part in out]
    out = pl.pallas_call(
        drain,
        out_shape=tuple(jax.ShapeDtypeStruct(part.shape, BF) for part in out),
        in_specs=[pl.BlockSpec(memory_space=pltpu.VMEM)] * 3,
        out_specs=(any_spec,) * 3,
        scratch_shapes=[pltpu.SemaphoreType.DMA((3,))],
        compiler_params=pltpu.CompilerParams(vmem_limit_bytes=1024 * 1024),
    )(*out)
    return out[0], out[1], jnp.swapaxes(out[2], 1, 2)


def solution(mesh):
    placed = (
        P("pair", "fsdp"),
        P("pair", "fsdp"),
        P("fsdp", None),
        P(None, "fsdp", None),
        P(None, None, "fsdp"),
        P("pair"),
        P(),
    )
    return jax.shard_map(
        per_device,
        mesh=mesh,
        in_specs=placed,
        out_specs=(P("pair", "fsdp"), P("pair", "fsdp", None), P("pair", None, "fsdp")),
        check_vma=False,
    )
```
